32 devices in a mesh: sec: 4 (over y, x), strip: 8 (over z, core).
Axes of the slice: x: 2, y: 2, z: 4, core: 2. Of those that a mesh axis runs over, the one named last changes fastest.
Arguments:
- features: bfloat16 [4, 96, 128, 128], P('sec', 'strip'), may hold values from -6 to 6
- offsets: int32 [4], replicated, may hold values from -2 to 2
- state: float32 [2, 4, 96, 128], P(None, 'sec', 'strip'), may hold values from -6 to 6
- w_first: bfloat16 [3, 3, 162, 128], replicated, may hold values from -0.15625 to 0.15625
- b_first: float32 [128], replicated, may hold values from -3 to 3
- w_second: bfloat16 [3, 3, 128, 128], replicated, may hold values from -0.1875 to 0.1875
- b_second: float32 [128], replicated, may hold values from -3 to 3
- w_third: bfloat16 [3, 3, 128, 2], replicated, may hold values from -0.1875 to 0.1875
Outputs:
- updated: float32 [2, 4, 96, 128], P(None, 'sec', 'strip')
The draws below stay inside these ranges and needn't reach their ends.
Inputs may be any that keep to these rules, and one draw needn't show every extreme that they name: offsets[s] is the integer row offset of section s+1 against section s; the last entry is not used.
All inputs are finite; a program needn't handle non-finite values.
Results may differ from the reference program's by a relative error of at most 0.0029.
Values may be sent and summed in bfloat16 or wider, within the bound.
A program may use at most 64 MiB of HBM per device.

```python
import jax
import jax.numpy as jnp
from jax import lax

C = 128
HID = 128
COLS = 128
SECTIONS = 4
ROWS = 96


def plant(result, key, low, high):
    spot = [jax.random.randint(jax.random.fold_in(key, axis), (), 0, length) for axis, length in enumerate(result.shape)]
    main_axis = result.shape.index(max(result.shape))
    beside = spot[:main_axis] + [(spot[main_axis] + 1) % result.shape[main_axis]] + spot[main_axis + 1:]
    return result.at[tuple(spot)].set(low).at[tuple(beside)].set(high)


def block_levels(key, dims, shards, least, top_value):
    def one(axis_at, blocks):
        heights = jax.random.uniform(jax.random.fold_in(jax.random.fold_in(key, 6), axis_at), (blocks,), jnp.float32, least / len(shards), top_value / len(shards))
        return jnp.repeat(jnp.exp(heights), dims[axis_at] // blocks).reshape((-1,) + (1,) * (len(dims) - axis_at - 1))

    loudness = one(*shards[0])
    for cut in shards[1:]:
        loudness = loudness * one(*cut)
    return loudness


def bell_draw(stream_key, shape, spread, most, split=(), held_as=jnp.bfloat16):
    drawn = spread * jax.random.normal(stream_key, shape, jnp.float32)
    if split:
        drawn = drawn * block_levels(stream_key, shape, split, -0.22, 0.18)
    return jnp.clip(drawn, -most, most).astype(held_as)


def setup_inputs(seed: int = 0) -> dict:
    seeds = jax.random.split(jax.random.key(seed), 9)
    features = bell_draw(seeds[0], (SECTIONS, ROWS, COLS, C), 1.0, 6.0, ((0, 4), (1, 8)))
    offsets = plant(jax.random.randint(seeds[1], (SECTIONS,), -2, 3), jax.random.fold_in(seeds[1], 1), -2, 2).astype(jnp.int32)
    state = bell_draw(seeds[2], (2, SECTIONS, ROWS, COLS), 1.0, 6.0, ((1, 4), (2, 8)), jnp.float32)
    w_first = bell_draw(seeds[3], (3, 3, 162, HID), (9 * 162) ** -0.5, 0.15625)
    b_first = bell_draw(seeds[4], (HID,), 0.5, 3.0, (), jnp.float32)
    w_second = bell_draw(seeds[5], (3, 3, HID, HID), (9 * HID) ** -0.5, 0.1875)
    b_second = bell_draw(seeds[6], (HID,), 0.5, 3.0, (), jnp.float32)
    w_third = bell_draw(seeds[7], (3, 3, HID, 2), (9 * HID) ** -0.5, 0.1875)
    return {"features": features, "offsets": offsets, "state": state, "w_first": w_first, "b_first": b_first, "w_second": w_second, "b_second": b_second, "w_third": w_third}


def corr_pair(mine, other, shift):
    padded = jnp.pad(other.astype(jnp.float32), ((6, 6), (4, 4), (0, 0)))
    mine_f = mine.astype(jnp.float32)
    planes = []
    for row_step in range(-4, 5):
        start = (6 + row_step + shift).astype(jnp.int32)
        taken = lax.dynamic_slice_in_dim(padded, start, ROWS, 0)
        for col_step in range(-4, 5):
            planes.append(jnp.sum(mine_f * taken[:, 4 + col_step:4 + col_step + COLS], axis=-1))
    return jnp.stack(planes)


def convolve(values, kernel, layout):
    return lax.conv_general_dilated(values[None], kernel, (1, 1), ((1, 1), (1, 1)),
                                    dimension_numbers=(layout, "HWIO", "NHWC"),
                                    preferred_element_type=jnp.float32)[0]


def reference(features, offsets, state, w_first, b_first, w_second, b_second, w_third):
    empty = jnp.zeros_like(features[:1])
    below_all = jnp.concatenate([empty, features[:-1]], 0)
    above_all = jnp.concatenate([features[1:], empty], 0)
    shift_above = offsets.astype(jnp.int32)
    shift_below = jnp.concatenate([jnp.zeros((1,), jnp.int32), -offsets[:-1].astype(jnp.int32)], 0)

    def one_section(items):
        mine, below, above, down_shift, up_shift = items
        corr = jnp.concatenate([corr_pair(mine, below, down_shift), corr_pair(mine, above, up_shift)], 0)
        corr = (corr * (C ** -0.5)).astype(jnp.bfloat16)
        hidden_one = jax.nn.relu(convolve(corr, w_first, "NCHW") + b_first).astype(jnp.bfloat16)
        hidden_two = jax.nn.relu(convolve(hidden_one, w_second, "NHWC") + b_second).astype(jnp.bfloat16)
        delta = convolve(hidden_two, w_third, "NHWC")
        return jnp.moveaxis(delta, 2, 0)

    deltas = lax.map(one_section, (features, below_all, above_all, shift_below, shift_above))
    return state + jnp.moveaxis(deltas, 1, 0)
```

```python
import functools

import jax
import jax.numpy as jnp
from jax import lax
from jax.experimental import pallas as pl
from jax.experimental.pallas import tpu as pltpu
from jax.sharding import PartitionSpec as P

SIDE = 9
STEP = 3
PAIR = 2
TAPS = 9
SPAN = TAPS + 1
LEFT = SPAN + STEP
EDGE = SIDE + 1
HALO = EDGE // PAIR
HBM = pl.BlockSpec(memory_space=pltpu.HBM)
VMEM = pl.BlockSpec(memory_space=pltpu.VMEM)
MESH = pl.DeviceIdType.MESH


def group_of(rows):
    return max(g for g in range(1, 8) if rows % g == 0)


def when(cond, act):
    if cond is None:
        act()
    else:
        pl.when(cond)(act)


def both(x, y):
    return y if x is None else x & y


def convolve(sources, weight, bias, target):
    rows, cols, width = target.shape
    depth = sources[0].shape[2]
    group = group_of(rows)
    at_col = lax.broadcasted_iota(jnp.int32, (cols, width), 0)

    def step(g, carry):
        base = g * group
        taken = jnp.concatenate(
            [s[pl.ds(base + d, group)].reshape(group * cols, depth) for d in range(3) for s in sources], axis=1
        )
        sums = jnp.dot(taken, weight[...], preferred_element_type=jnp.float32)
        for i in range(group):
            one = sums[i * cols:(i + 1) * cols]
            before = jnp.where(at_col == 0, 0.0, pltpu.roll(one[:, :width], 1, 0))
            after = jnp.where(at_col == cols - 1, 0.0, pltpu.roll(one[:, 2 * width:], cols - 1, 0))
            total = one[:, width:2 * width] + before + after + bias[...]
            target[base + i] = jnp.maximum(total, 0.0).astype(target.dtype)
        return carry

    lax.fori_loop(0, rows // group, step, 0)


def skewed(block, shift):
    rows, cols = block.shape
    pieces = []
    start = 0
    for top in range(0, rows, 8):
        if (shift + top) % cols + 7 > cols:
            if top > start:
                pieces.append(pltpu.roll(block[start:top], (shift + start) % cols, 1, stride=1, stride_axis=0))
            crossing = pltpu.roll(block[top:top + 8], (shift + top - 8) % cols, 1, stride=1, stride_axis=0)
            pieces.append(pltpu.roll(crossing, 8, 1))
            start = top + 8
    if start < rows:
        pieces.append(pltpu.roll(block[start:], (shift + start) % cols, 1, stride=1, stride_axis=0))
    return jnp.concatenate(pieces, axis=0)


def kernel(secs, strips, feat, offsets, w_one, b_one, w_two, b_two, w_three, out,
           mine, near, far, met, corr, hid_one, hid_two, held_one, held_two, held_three, bias_one, bias_two, moved,
           wide_one, wide_two, thirds, direct_recv, relay_recv, beyond_recv, beside_recv, own_recv, send_sem, local_sem):
    rows, cols, chans = feat.shape[1:]
    hid = w_two.shape[3]
    planes = w_one.shape[2] // 2
    count = rows // PAIR
    first = count - HALO
    sec, strip = lax.axis_index("sec"), lax.axis_index("strip")
    odd = lax.rem(sec, 2)
    partner = sec + 1 - 2 * odd
    relay_to, relay_from = sec + 2 - 4 * odd, sec - 2 + 4 * odd
    has_to = (relay_to >= 0) & (relay_to < secs)
    has_from = (relay_from >= 0) & (relay_from < secs)
    has_low, has_high = strip > 0, strip < strips - 1
    core = lax.rem(strip, 2)
    beyond, beside = strip - 1 + 2 * core, strip + 1 - 2 * core
    has_beyond = (beyond >= 0) & (beyond < strips)

    barrier = pltpu.get_barrier_semaphore()
    for cond, a, b in (
        (None, partner, strip), (has_from, relay_from, strip), (None, sec, beside), (has_beyond, sec, beyond),
    ):
        when(cond, lambda a=a, b=b: pl.semaphore_signal(barrier, inc=1, device_id=(a, b), device_id_type=MESH))

    loads = [
        pltpu.make_async_copy(src, dst, local_sem.at[i])
        for i, (src, dst) in enumerate((
            (feat.at[0], mine.at[pl.ds(LEFT + STEP, rows)]), (w_one, held_one), (w_two, held_two), (w_three, held_three),
            (b_one, bias_one), (b_two, bias_two), (offsets, moved),
        ))
    ]
    for load in loads:
        load.start()
    pl.semaphore_wait(barrier, 2 + has_to.astype(jnp.int32) + has_beyond.astype(jnp.int32))

    def remote(src, dst, send, recv, a, b):
        return pltpu.make_async_remote_copy(
            src_ref=src, dst_ref=dst, send_sem=send_sem.at[send], recv_sem=recv, device_id=(a, b), device_id_type=MESH
        )

    def top_of(k):
        return jnp.where(core == 0, PAIR * k, rows - PAIR - PAIR * k)

    def direct(k):
        at = top_of(k)
        return remote(feat.at[0, pl.ds(at, PAIR)], near.at[pl.ds(EDGE + at, PAIR)], 0, direct_recv.at[k], partner, strip)

    def relay(k):
        at = pl.ds(EDGE + top_of(k), PAIR)
        return remote(near.at[at], far.at[at], 1, relay_recv.at[k], relay_to, strip)

    def to_beyond(slot, s, k, length):
        at = top_of(k) + core * (PAIR - length)
        to = EDGE + at + rows - 2 * rows * core
        return remote(
            slot.at[pl.ds(EDGE + at, length)], slot.at[pl.ds(to, length)], 2 + s, beyond_recv.at[s, k], sec, beyond
        )

    def to_beside(slot, s, k, length):
        at = top_of(k) + (1 - core) * (PAIR - length)
        to = EDGE + at - rows + 2 * rows * core
        return remote(
            slot.at[pl.ds(EDGE + at, length)], slot.at[pl.ds(to, length)], 4 + s, beside_recv.at[s, k - first], sec, beside
        )

    def each_start(k, carry):
        direct(k).start()
        return carry

    lax.fori_loop(0, count, each_start, 0)
    own_low = remote(feat.at[0, pl.ds(0, STEP)], mine.at[pl.ds(LEFT + STEP + rows, STEP)], 6, own_recv.at[0], sec, strip - 1)
    own_high = remote(feat.at[0, pl.ds(rows - STEP, STEP)], mine.at[pl.ds(LEFT, STEP)], 7, own_recv.at[1], sec, strip + 1)
    when(has_low, own_low.start)
    when(has_high, own_high.start)

    zero = jnp.zeros((LEFT,) + mine.shape[1:], mine.dtype)
    mine[0:LEFT] = zero
    mine[LEFT + rows + 2 * STEP:] = zero
    for slot in (near, far):
        slot[0] = zero[0]
        slot[slot.shape[0] - 1] = zero[0]

    @pl.when(jnp.logical_not(has_low))
    def _():
        mine[LEFT:LEFT + STEP] = zero[:STEP]

    @pl.when(jnp.logical_not(has_high))
    def _():
        mine[LEFT + STEP + rows:LEFT + 2 * STEP + rows] = zero[:STEP]

    @pl.when(jnp.logical_not(has_beyond))
    def _():
        for s in range(2):
            met[s, pl.ds(core * (EDGE + rows), EDGE)] = jnp.zeros((EDGE, cols, cols), met.dtype)

    scale = chans ** (-0.5)
    lane = lax.broadcasted_iota(jnp.int32, (cols, cols), 1)
    col = lax.broadcasted_iota(jnp.int32, (cols, cols), 0)
    flip = (lane + col == cols - 1).astype(mine.dtype)
    other = cols - 1 - col + lax.rem(lane, TAPS) - 4
    gain = jnp.where((other >= 0) & (other < cols) & (lane < planes), scale, 0.0)

    def turn(r, carry):
        mine[r] = jnp.dot(flip, mine[r], preferred_element_type=jnp.float32).astype(mine.dtype)
        return carry

    for load in loads:
        load.wait()
    lax.fori_loop(LEFT + STEP, LEFT + STEP + rows, turn, 0)
    for d in range(3):
        thirds[8 * d:8 * d + 8] = jnp.zeros((8, hid), thirds.dtype)
        for e in range(3):
            thirds[8 * d + 4 - 2 * e:8 * d + 6 - 2 * e] = held_three[d, e].astype(thirds.dtype)
    for d in range(2 * 3):
        wide_one[d * cols + planes // 16 * 16:(d + 1) * cols] = jnp.zeros((cols - planes // 16 * 16, 3 * hid), wide_one.dtype)
    for d in range(3):
        for e in range(3):
            at = pl.ds((2 - e) * hid, hid)
            for j in range(2):
                wide_one[pl.ds((2 * d + j) * cols, planes), at] = held_one[d, e, j * planes:(j + 1) * planes]
            wide_two[pl.ds(d * hid, hid), at] = held_two[d, e]

    when(has_low, own_high.wait_recv)
    when(has_high, own_low.wait_recv)
    lax.fori_loop(LEFT, LEFT + STEP, turn, 0)
    lax.fori_loop(LEFT + STEP + rows, LEFT + 2 * STEP + rows, turn, 0)

    below = jnp.where(sec > 0, -moved[jnp.maximum(sec - 1, 0)], 0)
    above = jnp.where(sec < secs - 1, moved[sec], 0)
    shifts = (jnp.where(odd == 1, below, above), jnp.where(odd == 1, above, below))
    slots = (near, far)

    def meet(s, w):
        here = mine[pl.ds(w + LEFT - SPAN - 1 - shifts[s], SPAN)].reshape(SPAN * cols, chans)
        there = slots[s][pl.ds(w, PAIR)].reshape(PAIR * cols, chans)
        tile = lax.dot_general(here, there, (((1,), (1,)), ((), ())), preferred_element_type=jnp.float32)
        for u in range(PAIR):
            def block(t):
                j = TAPS - 1 - t + u
                return skewed(tile[j * cols:(j + 1) * cols, u * cols:(u + 1) * cols], t * TAPS + 5)

            found = block(0)
            for t in range(1, TAPS):
                found = jnp.where(lane >= t * TAPS, block(t), found)
            met[s, w + u] = (found * gain).astype(met.dtype)

    def forward(s, k):
        slot = slots[s]
        when(has_beyond & (k < HALO - 1), lambda: to_beyond(slot, s, k, PAIR).start())
        when(has_beyond & (k == HALO - 1), lambda: to_beyond(slot, s, k, PAIR - 1).start())
        when(k > first, lambda: to_beside(slot, s, k, PAIR).start())
        when(k == first, lambda: to_beside(slot, s, k, PAIR - 1).start())

    def from_beyond(s, k):
        when(k < HALO - 1, lambda: to_beyond(slots[s], s, k, PAIR).wait_recv())
        when(k == HALO - 1, lambda: to_beyond(slots[s], s, k, PAIR - 1).wait_recv())
        meet(s, jnp.where(core == 0, EDGE - PAIR - PAIR * k, EDGE + rows + PAIR * k))

    def from_beside(s, k):
        when(k > first, lambda: to_beside(slots[s], s, k, PAIR).wait_recv())
        when(k == first, lambda: to_beside(slots[s], s, k, PAIR - 1).wait_recv())
        meet(s, jnp.where(core == 0, EDGE + 2 * rows - PAIR - PAIR * k, EDGE - rows + PAIR * k))

    def stage(i, carry):
        @pl.when(i < count)
        def _():
            direct(i).wait_recv()
            when(has_to, lambda: relay(i).start())
            forward(0, i)
            meet(0, EDGE + top_of(i))

        when((i - 1 >= first) & (i - 1 < count), lambda: from_beside(0, i - 1))
        when(has_beyond & (i - 2 >= 0) & (i - 2 < HALO), lambda: from_beyond(0, i - 2))

        @pl.when(has_from & (i - 1 >= 0) & (i - 1 < count))
        def _():
            relay(i - 1).wait_recv()
            forward(1, i - 1)
            meet(1, EDGE + top_of(i - 1))

        when(has_from & (i - 3 >= first) & (i - 3 < count), lambda: from_beside(1, i - 3))
        when(has_from & has_beyond & (i - 4 >= 0) & (i - 4 < HALO), lambda: from_beyond(1, i - 4))
        return carry

    lax.fori_loop(0, max(count + 3, HALO + 4), stage, 0)

    def gather(s, at):
        def one(e, carry):
            found = met[s, e + STEP + shifts[s]]
            for a in range(1, TAPS):
                found = jnp.where(lane >= a * TAPS, met[s, e + STEP + shifts[s] + a], found)
            corr[at, e] = found
            return carry

        lax.fori_loop(0, rows + 2 * STEP, one, 0)

    gather(0, 1 - odd)
    when(has_from, lambda: gather(1, odd))

    @pl.when(jnp.logical_not(has_from))
    def _():
        corr[odd] = jnp.zeros(corr.shape[1:], corr.dtype)

    convolve((corr.at[0], corr.at[1]), wide_one, bias_one, hid_one)

    @pl.when(strip == 0)
    def _():
        hid_one[0:2] = jnp.zeros((2, cols, hid), hid_one.dtype)

    @pl.when(strip == strips - 1)
    def _():
        hid_one[rows + 2:] = jnp.zeros((2, cols, hid), hid_one.dtype)

    convolve((hid_one,), wide_two, bias_two, hid_two)

    @pl.when(strip == 0)
    def _():
        hid_two[0:1] = jnp.zeros((1, cols, hid), hid_two.dtype)

    @pl.when(strip == strips - 1)
    def _():
        hid_two[rows + 1:] = jnp.zeros((1, cols, hid), hid_two.dtype)

    taps = lax.dot_general(
        thirds[...].astype(hid_two.dtype), hid_two[...].reshape((rows + 2) * cols, hid), (((1,), (1,)), ((), ())),
        preferred_element_type=jnp.float32,
    )
    at_lane = lax.broadcasted_iota(jnp.int32, (8, cols), 1)
    found = []
    for r in range(rows):
        total = sum(taps[8 * d:8 * d + 8, (r + d) * cols:(r + d + 1) * cols] for d in range(3))
        before = jnp.where(at_lane == 0, 0.0, pltpu.roll(total, 1, 1))
        after = jnp.where(at_lane == cols - 1, 0.0, pltpu.roll(total, cols - 1, 1))
        found.append(before[0:2] + total[2:4] + after[4:6])
    turned = jnp.dot(
        jnp.concatenate(found, axis=0), flip.astype(jnp.float32),
        preferred_element_type=jnp.float32, precision=lax.Precision.HIGHEST,
    )
    for r in range(rows):
        for p in range(2):
            out[p * rows + r] = turned[2 * r + p:2 * r + p + 1]

    def sent(slot, length, send, a, b):
        at = pl.ds(EDGE, length)
        return remote(slot.at[at], slot.at[at], send, direct_recv.at[0], a, b).wait_send

    sent(near, rows, 0, partner, strip)()
    when(has_to, sent(near, rows, 1, relay_to, strip))
    for s, known in ((0, None), (1, has_from)):
        when(both(known, has_beyond), sent(slots[s], SIDE, 2 + s, sec, beyond))
        when(known, sent(slots[s], SIDE, 4 + s, sec, beside))
    when(has_low, own_low.wait_send)
    when(has_high, own_high.wait_send)


def body(secs, strips, features, offsets, state, w_first, b_first, w_second, b_second, w_third):
    _, rows, cols, chans = features.shape
    hid = w_first.shape[3]
    parts = w_third.shape[3]
    bf16 = jnp.bfloat16
    count = rows // PAIR
    thirds = jnp.transpose(w_third, (0, 1, 3, 2))
    dma = pltpu.SemaphoreType.DMA
    delta = pl.pallas_call(
        functools.partial(kernel, secs, strips),
        out_shape=jax.ShapeDtypeStruct((parts * rows, 1, cols), jnp.float32),
        in_specs=[HBM] * 7,
        out_specs=VMEM,
        scratch_shapes=[
            pltpu.VMEM((rows + 2 * STEP + 2 * LEFT, cols, chans), bf16),
            pltpu.VMEM((rows + 2 * EDGE, cols, chans), bf16),
            pltpu.VMEM((rows + 2 * EDGE, cols, chans), bf16),
            pltpu.VMEM((2, rows + 2 * EDGE, cols, cols), bf16),
            pltpu.VMEM((2, rows + 2 * STEP, cols, cols), bf16),
            pltpu.VMEM((rows + 4, cols, hid), bf16),
            pltpu.VMEM((rows + 2, cols, hid), bf16),
            pltpu.VMEM(w_first.shape, bf16),
            pltpu.VMEM(w_second.shape, bf16),
            pltpu.VMEM(thirds.shape, bf16),
            pltpu.VMEM((1, hid), jnp.float32),
            pltpu.VMEM((1, hid), jnp.float32),
            pltpu.SMEM(offsets.shape, jnp.int32),
            pltpu.VMEM((6 * cols, 3 * hid), bf16),
            pltpu.VMEM((3 * hid, 3 * hid), bf16),
            pltpu.VMEM((24, hid), jnp.float32),
            dma((count,)),
            dma((count,)),
            dma((2, HALO)),
            dma((2, HALO)),
            dma((2,)),
            dma((8,)),
            dma((7,)),
        ],
        compiler_params=pltpu.CompilerParams(collective_id=0, has_side_effects=True, vmem_limit_bytes=24 << 20),
    )(features, offsets, w_first, b_first.reshape(1, hid), w_second, b_second.reshape(1, hid), thirds)
    return state + delta.reshape(state.shape)


def solution(mesh):
    secs, strips = mesh.shape["sec"], mesh.shape["strip"]
    in_specs = (
        P("sec", "strip", None, None),
        P(),
        P(None, "sec", "strip", None),
        P(),
        P(),
        P(),
        P(),
        P(),
    )
    out_specs = P(None, "sec", "strip", None)
    return jax.shard_map(functools.partial(body, secs, strips), mesh=mesh, in_specs=in_specs, out_specs=out_specs, check_vma=False)
```

```python
import functools

import jax
import jax.numpy as jnp
from jax import lax
from jax.experimental import pallas as pl
from jax.experimental.pallas import tpu as pltpu
from jax.sharding import PartitionSpec as P

SIDE = 9
STEP = 3
PAIR = 2
TAPS = 9
SPAN = TAPS + 1
LEFT = SPAN + STEP
EDGE = SIDE + 1
HALO = EDGE // PAIR
WINDOW = 16
SLOTS = 8
QUAD = 2 * PAIR
RELAYED = 2
BITS = 4
HBM = pl.BlockSpec(memory_space=pltpu.HBM)
VMEM = pl.BlockSpec(memory_space=pltpu.VMEM)
MESH = pl.DeviceIdType.MESH


def group_of(rows):
    return max(g for g in range(1, 8) if rows % g == 0)


def when(cond, act):
    if cond is None:
        act()
    else:
        pl.when(cond)(act)


def both(x, y):
    return y if x is None else x & y


def plan(rows):
    count = rows // PAIR
    tasks = {}
    for w in range(0, rows + 2 * EDGE, QUAD):
        ready = []
        for at in (w, w + PAIR):
            if at < EDGE:
                ready.append((EDGE - PAIR - at) // PAIR + 2)
            elif at >= EDGE + rows:
                ready.append((EDGE + 2 * rows - PAIR - at) // PAIR + 1)
            else:
                ready.append((at - EDGE) // PAIR)
        tasks.setdefault(max(ready), []).append(w // QUAD + 1)
    stages = max(max(tasks) + 1, count)
    width = max(len(found) for found in tasks.values())
    return [[(tasks.get(i, []) + [0] * width)[q] for i in range(stages)] for q in range(width)]


def convolve(sources, weight, bias, target):
    rows, cols, width = target.shape
    depth = sources[0].shape[2]
    group = group_of(rows)
    at_col = lax.broadcasted_iota(jnp.int32, (cols, width), 0)

    def step(g, carry):
        base = g * group
        taken = jnp.concatenate(
            [s[pl.ds(base + d, group)].reshape(group * cols, depth) for d in range(3) for s in sources], axis=1
        )
        sums = jnp.dot(taken, weight[...], preferred_element_type=jnp.float32)
        for i in range(group):
            one = sums[i * cols:(i + 1) * cols]
            before = jnp.where(at_col == 0, 0.0, pltpu.roll(one[:, :width], 1, 0))
            after = jnp.where(at_col == cols - 1, 0.0, pltpu.roll(one[:, 2 * width:], cols - 1, 0))
            total = one[:, width:2 * width] + before + after + bias[...]
            target[base + i] = jnp.maximum(total, 0.0).astype(target.dtype)
        return carry

    lax.fori_loop(0, rows // group, step, 0)


def kernel(secs, strips, feat, offsets, w_one, b_one, w_two, b_two, w_three, out,
           mine, wide, met, twin, corr, hid_one, hid_two, held_one, held_two, held_three, bias_one, bias_two, moved,
           wide_one, wide_two, thirds, direct_recv, relay_recv, beyond_recv, beside_recv, own_recv, send_sem, local_sem):
    rows, cols, chans = feat.shape[1:]
    hid = w_two.shape[3]
    planes = w_one.shape[2] // 2
    count = rows // PAIR
    first = count - HALO
    sec, strip = lax.axis_index("sec"), lax.axis_index("strip")
    odd = lax.rem(sec, 2)
    partner = sec + 1 - 2 * odd
    relay_to, relay_from = sec + 2 - 4 * odd, sec - 2 + 4 * odd
    has_to = (relay_to >= 0) & (relay_to < secs)
    has_from = (relay_from >= 0) & (relay_from < secs)
    has_low, has_high = strip > 0, strip < strips - 1
    core = lax.rem(strip, 2)
    beyond, beside = strip - 1 + 2 * core, strip + 1 - 2 * core
    has_beyond = (beyond >= 0) & (beyond < strips)

    barrier = pltpu.get_barrier_semaphore()
    for cond, a, b in (
        (None, partner, strip), (has_from, relay_from, strip), (None, sec, beside), (has_beyond, sec, beyond),
    ):
        when(cond, lambda a=a, b=b: pl.semaphore_signal(barrier, inc=1, device_id=(a, b), device_id_type=MESH))

    loads = [
        pltpu.make_async_copy(src, dst, local_sem.at[i])
        for i, (src, dst) in enumerate((
            (feat.at[0], mine.at[pl.ds(LEFT + STEP, rows)]), (w_one, held_one), (w_two, held_two), (w_three, held_three),
            (b_one, bias_one), (b_two, bias_two), (offsets, moved),
        ))
    ]
    for load in loads:
        load.start()
    pl.semaphore_wait(barrier, 2 + has_to.astype(jnp.int32) + has_beyond.astype(jnp.int32))

    def remote(src, dst, send, recv, a, b):
        return pltpu.make_async_remote_copy(
            src_ref=src, dst_ref=dst, send_sem=send_sem.at[send], recv_sem=recv, device_id=(a, b), device_id_type=MESH
        )

    def top_of(k):
        return jnp.where(core == 0, PAIR * k, rows - PAIR - PAIR * k)

    def direct(k):
        at = top_of(k)
        return remote(feat.at[0, pl.ds(at, PAIR)], wide.at[0, pl.ds(EDGE + at, PAIR)], 0, direct_recv.at[k], partner, strip)

    def relay(k):
        at = pl.ds(EDGE + top_of(k), PAIR)
        return remote(wide.at[0, at], wide.at[1, at], 1, relay_recv.at[k], relay_to, strip)

    def to_beyond(s, k, length):
        at = top_of(k) + core * (PAIR - length)
        to = EDGE + at + rows - 2 * rows * core
        return remote(
            wide.at[s, pl.ds(EDGE + at, length)], wide.at[s, pl.ds(to, length)], 2 + s, beyond_recv.at[s, k], sec, beyond
        )

    def to_beside(s, k, length):
        at = top_of(k) + (1 - core) * (PAIR - length)
        to = EDGE + at - rows + 2 * rows * core
        return remote(
            wide.at[s, pl.ds(EDGE + at, length)], wide.at[s, pl.ds(to, length)], 4 + s, beside_recv.at[s, k - first], sec, beside
        )

    def each_start(k, carry):
        direct(k).start()
        return carry

    lax.fori_loop(0, count, each_start, 0)
    own_low = remote(feat.at[0, pl.ds(0, STEP)], mine.at[pl.ds(LEFT + STEP + rows, STEP)], 6, own_recv.at[0], sec, strip - 1)
    own_high = remote(feat.at[0, pl.ds(rows - STEP, STEP)], mine.at[pl.ds(LEFT, STEP)], 7, own_recv.at[1], sec, strip + 1)
    when(has_low, own_low.start)
    when(has_high, own_high.start)

    zero = jnp.zeros((LEFT,) + mine.shape[1:], mine.dtype)
    mine[0:LEFT] = zero
    mine[LEFT + rows + 2 * STEP:] = zero
    for s in range(2):
        wide[s, 0] = zero[0]
        wide[s, wide.shape[1] - 1] = zero[0]

    @pl.when(jnp.logical_not(has_low))
    def _():
        mine[LEFT:LEFT + STEP] = zero[:STEP]

    @pl.when(jnp.logical_not(has_high))
    def _():
        mine[LEFT + STEP + rows:LEFT + 2 * STEP + rows] = zero[:STEP]

    @pl.when(jnp.logical_not(has_beyond))
    def _():
        for s in range(2):
            wide[s, pl.ds(core * (EDGE + rows), EDGE)] = jnp.zeros((EDGE, cols, chans), wide.dtype)

    scale = chans ** (-0.5)
    lane = lax.broadcasted_iota(jnp.int32, (cols, cols), 1)
    col = lax.broadcasted_iota(jnp.int32, (cols, cols), 0)
    plane = lax.div(lane, TAPS)
    across = lax.rem(lane, TAPS) - 4
    other = col + across
    inside = (other >= 0) & (other < cols) & (lane < planes)
    source = other + WINDOW * plane
    offset = lane - lax.div(col, 8) * 8 + 4

    for load in loads:
        load.wait()
    for d in range(3):
        thirds[8 * d:8 * d + 8] = jnp.zeros((8, hid), thirds.dtype)
        for e in range(3):
            thirds[8 * d + 2 * e:8 * d + 2 * e + 2] = held_three[d, e].astype(thirds.dtype)
    for d in range(2 * 3):
        wide_one[d * cols + planes // 16 * 16:(d + 1) * cols] = jnp.zeros((cols - planes // 16 * 16, 3 * hid), wide_one.dtype)
    for d in range(3):
        for e in range(3):
            at = pl.ds(e * hid, hid)
            for j in range(2):
                wide_one[pl.ds((2 * d + j) * cols, planes), at] = held_one[d, e, j * planes:(j + 1) * planes]
            wide_two[pl.ds(d * hid, hid), at] = held_two[d, e]

    when(has_low, own_high.wait_recv)
    when(has_high, own_low.wait_recv)

    below = jnp.where(sec > 0, -moved[jnp.maximum(sec - 1, 0)], 0)
    above = jnp.where(sec < secs - 1, moved[sec], 0)
    shifts = (jnp.where(odd == 1, below, above), jnp.where(odd == 1, above, below))

    def meet(s, w):
        shift = jnp.where(s == 0, shifts[0], shifts[1])
        for u in range(QUAD):
            row = wide[s, w + u]
            twin[u, 0:cols] = row
            twin[u, cols:] = row
        turned = [
            twin[u, pl.ds(pl.multiple_of(cols - WINDOW * lax.rem(w + u, SLOTS), WINDOW), cols)] for u in range(QUAD)
        ]
        slot = lax.rem(w, 2 * SLOTS)
        side = slot // SLOTS
        place = (offset - WINDOW * slot) & (cols - 1)
        here = mine[pl.ds(w + LEFT - SPAN - 1 - shift, SPAN + PAIR)]
        tiles = []
        for v in range(2):
            own = here[v * PAIR:v * PAIR + SPAN].reshape(SPAN * cols, chans)
            there = jnp.concatenate(turned[v * PAIR:(v + 1) * PAIR], axis=0)
            tiles.append(lax.dot_general(own, there, (((1,), (1,)), ((), ())), preferred_element_type=jnp.float32))
        for j in range(SPAN + PAIR):
            kept = met[s, side, w + j]
            for v in range(2):
                r = j - v * PAIR
                if 0 <= r < SPAN:
                    one = tiles[v][r * cols:(r + 1) * cols]
                    for u in range(PAIR):
                        if 0 <= TAPS - 1 - r + u < TAPS:
                            low = WINDOW * (v * PAIR + u)
                            kept = jnp.where((place >= low) & (place < low + WINDOW), one[:, u * cols:(u + 1) * cols], kept)
            met[s, side, w + j] = kept

    def gather(s, at):
        def one(g, carry):
            for i in range(STEP):
                e = g * STEP + i
                start = e + STEP + shifts[s]
                index = (source + WINDOW * start) & (cols - 1)
                upper = ((plane + start) & (2 * SLOTS - 1)) >= SLOTS
                own = e + SPAN + 1 + shifts[s]
                sides = [
                    jnp.take_along_axis(met[s, h, own], index, axis=1, mode="promise_in_bounds") for h in range(2)
                ]
                corr[at, e] = jnp.where(inside, jnp.where(upper, sides[1], sides[0]) * scale, 0.0).astype(corr.dtype)
            return carry

        lax.fori_loop(0, (rows + 2 * STEP) // STEP, one, 0)

    def halo(s, at):
        k_beyond = (EDGE - PAIR - at) // PAIR
        k_beside = (EDGE + 2 * rows - PAIR - at) // PAIR
        low, high = (at < EDGE) & has_beyond, at >= EDGE + rows
        when(low & (k_beyond < HALO - 1), lambda: to_beyond(s, k_beyond, PAIR).wait_recv())
        when(low & (k_beyond == HALO - 1), lambda: to_beyond(s, k_beyond, PAIR - 1).wait_recv())
        when(high & (k_beside > first), lambda: to_beside(s, k_beside, PAIR).wait_recv())
        when(high & (k_beside == first), lambda: to_beside(s, k_beside, PAIR - 1).wait_recv())

    table = plan(rows)
    stages, width = len(table[0]), len(table)
    codes = [sum(v << (BITS * i) for i, v in enumerate(line)) for line in table]

    def step(n, carry):
        q = lax.rem(n, width)
        m = n // width
        s = lax.rem(m, 2)
        j = m // 2
        k = j - RELAYED * s
        known = (s == 0) | has_from

        @pl.when(known & (q == 0) & (k >= 0) & (k < count))
        def _():
            when(s == 0, lambda: direct(k).wait_recv())
            when(s == 1, lambda: relay(k).wait_recv())
            when((s == 0) & has_to, lambda: relay(k).start())
            when(has_beyond & (k < HALO - 1), lambda: to_beyond(s, k, PAIR).start())
            when(has_beyond & (k == HALO - 1), lambda: to_beyond(s, k, PAIR - 1).start())
            when(k > first, lambda: to_beside(s, k, PAIR).start())
            when(k == first, lambda: to_beside(s, k, PAIR - 1).start())

        code = codes[0]
        for i in range(1, width):
            code = jnp.where(q == i, codes[i], code)
        task = lax.shift_right_logical(jnp.int32(code), BITS * jnp.clip(k, 0, stages - 1)) & (2 ** BITS - 1)

        @pl.when(known & (k >= 0) & (k < stages) & (task > 0))
        def _():
            w = QUAD * (task - 1)
            halo(s, w)
            halo(s, w + PAIR)
            meet(s, jnp.where(core == 0, w, rows + 2 * EDGE - QUAD - w))

        when((s == 0) & (q == 0) & (j == stages), lambda: gather(0, 1 - odd))
        return carry

    lax.fori_loop(0, (stages + RELAYED) * 2 * width, step, 0)

    when(has_from, lambda: gather(1, odd))

    @pl.when(jnp.logical_not(has_from))
    def _():
        corr[odd] = jnp.zeros(corr.shape[1:], corr.dtype)

    convolve((corr.at[0], corr.at[1]), wide_one, bias_one, hid_one)

    @pl.when(strip == 0)
    def _():
        hid_one[0:2] = jnp.zeros((2, cols, hid), hid_one.dtype)

    @pl.when(strip == strips - 1)
    def _():
        hid_one[rows + 2:] = jnp.zeros((2, cols, hid), hid_one.dtype)

    convolve((hid_one,), wide_two, bias_two, hid_two)

    @pl.when(strip == 0)
    def _():
        hid_two[0:1] = jnp.zeros((1, cols, hid), hid_two.dtype)

    @pl.when(strip == strips - 1)
    def _():
        hid_two[rows + 1:] = jnp.zeros((1, cols, hid), hid_two.dtype)

    taps = lax.dot_general(
        thirds[...].astype(hid_two.dtype), hid_two[...].reshape((rows + 2) * cols, hid), (((1,), (1,)), ((), ())),
        preferred_element_type=jnp.float32,
    )
    at_lane = lax.broadcasted_iota(jnp.int32, (8, cols), 1)
    found = []
    for r in range(rows):
        total = sum(taps[8 * d:8 * d + 8, (r + d) * cols:(r + d + 1) * cols] for d in range(3))
        before = jnp.where(at_lane == 0, 0.0, pltpu.roll(total, 1, 1))
        after = jnp.where(at_lane == cols - 1, 0.0, pltpu.roll(total, cols - 1, 1))
        found.append(before[0:2] + total[2:4] + after[4:6])
    turned = jnp.concatenate(found, axis=0)
    for r in range(rows):
        for p in range(2):
            out[p * rows + r] = turned[2 * r + p:2 * r + p + 1]

    def sent(s, length, send, a, b):
        at = pl.ds(EDGE, length)
        return remote(wide.at[s, at], wide.at[s, at], send, direct_recv.at[0], a, b).wait_send

    sent(0, rows, 0, partner, strip)()
    when(has_to, sent(0, rows, 1, relay_to, strip))
    for s, known in ((0, None), (1, has_from)):
        when(both(known, has_beyond), sent(s, SIDE, 2 + s, sec, beyond))
        when(known, sent(s, SIDE, 4 + s, sec, beside))
    when(has_low, own_low.wait_send)
    when(has_high, own_high.wait_send)


def body(secs, strips, features, offsets, state, w_first, b_first, w_second, b_second, w_third):
    _, rows, cols, chans = features.shape
    hid = w_first.shape[3]
    parts = w_third.shape[3]
    bf16 = jnp.bfloat16
    count = rows // PAIR
    thirds = jnp.transpose(w_third, (0, 1, 3, 2))
    dma = pltpu.SemaphoreType.DMA
    delta = pl.pallas_call(
        functools.partial(kernel, secs, strips),
        out_shape=jax.ShapeDtypeStruct((parts * rows, 1, cols), jnp.float32),
        in_specs=[HBM] * 7,
        out_specs=VMEM,
        scratch_shapes=[
            pltpu.VMEM((rows + 2 * STEP + 2 * LEFT, cols, chans), bf16),
            pltpu.VMEM((2, rows + 2 * EDGE, cols, chans), bf16),
            pltpu.VMEM((2, 2, rows + 2 * EDGE + SPAN, cols, cols), jnp.float32),
            pltpu.VMEM((QUAD, 2 * cols, chans), bf16),
            pltpu.VMEM((2, rows + 2 * STEP, cols, cols), bf16),
            pltpu.VMEM((rows + 4, cols, hid), bf16),
            pltpu.VMEM((rows + 2, cols, hid), bf16),
            pltpu.VMEM(w_first.shape, bf16),
            pltpu.VMEM(w_second.shape, bf16),
            pltpu.VMEM(thirds.shape, bf16),
            pltpu.VMEM((1, hid), jnp.float32),
            pltpu.VMEM((1, hid), jnp.float32),
            pltpu.SMEM(offsets.shape, jnp.int32),
            pltpu.VMEM((6 * cols, 3 * hid), bf16),
            pltpu.VMEM((3 * hid, 3 * hid), bf16),
            pltpu.VMEM((24, hid), jnp.float32),
            dma((count,)),
            dma((count,)),
            dma((2, HALO)),
            dma((2, HALO)),
            dma((2,)),
            dma((8,)),
            dma((7,)),
        ],
        compiler_params=pltpu.CompilerParams(collective_id=0, has_side_effects=True, vmem_limit_bytes=56 << 20),
    )(features, offsets, w_first, b_first.reshape(1, hid), w_second, b_second.reshape(1, hid), thirds)
    return state + delta.reshape(state.shape)


def solution(mesh):
    secs, strips = mesh.shape["sec"], mesh.shape["strip"]
    in_specs = (
        P("sec", "strip", None, None),
        P(),
        P(None, "sec", "strip", None),
        P(),
        P(),
        P(),
        P(),
        P(),
    )
    out_specs = P(None, "sec", "strip", None)
    return jax.shard_map(functools.partial(body, secs, strips), mesh=mesh, in_specs=in_specs, out_specs=out_specs, check_vma=False)
```

```python
import functools

import jax
import jax.numpy as jnp
from jax import lax
from jax.experimental import pallas as pl
from jax.experimental.pallas import tpu as pltpu
from jax.sharding import PartitionSpec as P

SIDE = 9
STEP = 3
PAIR = 2
TAPS = 9
SPAN = TAPS + 1
LEFT = SPAN + STEP
EDGE = SIDE + 1
HALO = EDGE // PAIR
QUAD = 2 * PAIR
RELAYED = 2
BITS = 4
HBM = pl.BlockSpec(memory_space=pltpu.HBM)
VMEM = pl.BlockSpec(memory_space=pltpu.VMEM)
MESH = pl.DeviceIdType.MESH


def group_of(rows):
    return max(g for g in range(1, 9) if rows % g == 0)


def when(cond, act):
    if cond is None:
        act()
    else:
        pl.when(cond)(act)


def both(x, y):
    return y if x is None else x & y


def plan(rows):
    count = rows // PAIR
    tasks = {}
    for w in range(0, rows + 2 * EDGE, QUAD):
        ready = []
        for at in (w, w + PAIR):
            if at < EDGE:
                ready.append((EDGE - PAIR - at) // PAIR + 2)
            elif at >= EDGE + rows:
                ready.append((EDGE + 2 * rows - PAIR - at) // PAIR + 1)
            else:
                ready.append((at - EDGE) // PAIR)
        tasks.setdefault(max(ready), []).append(w // QUAD + 1)
    stages = max(max(tasks) + 1, count)
    width = max(len(found) for found in tasks.values())
    return [[(tasks.get(i, []) + [0] * width)[q] for i in range(stages)] for q in range(width)]


def convolve(sources, weight, bias, target):
    rows, cols, width = target.shape
    depth = sources[0].shape[2]
    group = group_of(rows)
    at_col = lax.broadcasted_iota(jnp.int32, (cols, width), 0)

    def step(g, carry):
        base = g * group
        taken = jnp.concatenate(
            [s[pl.ds(base + d, group)].reshape(group * cols, depth) for d in range(3) for s in sources], axis=1
        )
        sums = jnp.dot(taken, weight[...], preferred_element_type=jnp.float32)
        for i in range(group):
            one = sums[i * cols:(i + 1) * cols]
            before = jnp.where(at_col == 0, 0.0, pltpu.roll(one[:, :width], 1, 0))
            after = jnp.where(at_col == cols - 1, 0.0, pltpu.roll(one[:, 2 * width:], cols - 1, 0))
            total = one[:, width:2 * width] + before + after + bias[...]
            target[base + i] = jnp.maximum(total, 0.0).astype(target.dtype)
        return carry

    lax.fori_loop(0, rows // group, step, 0)


def kernel(secs, strips, feat, offsets, w_one, b_one, w_two, b_two, w_three, out,
           mine, wide, met, corr, hid_one, hid_two, held_one, held_two, held_three, bias_one, bias_two, moved,
           wide_one, wide_two, thirds, direct_recv, relay_recv, beyond_recv, beside_recv, own_recv, send_sem, local_sem):
    rows, cols, chans = feat.shape[1:]
    hid = w_two.shape[3]
    planes = w_one.shape[2] // 2
    count = rows // PAIR
    first = count - HALO
    sec, strip = lax.axis_index("sec"), lax.axis_index("strip")
    odd = lax.rem(sec, 2)
    partner = sec + 1 - 2 * odd
    relay_to, relay_from = sec + 2 - 4 * odd, sec - 2 + 4 * odd
    has_to = (relay_to >= 0) & (relay_to < secs)
    has_from = (relay_from >= 0) & (relay_from < secs)
    has_low, has_high = strip > 0, strip < strips - 1
    core = lax.rem(strip, 2)
    beyond, beside = strip - 1 + 2 * core, strip + 1 - 2 * core
    has_beyond = (beyond >= 0) & (beyond < strips)

    barrier = pltpu.get_barrier_semaphore()
    for cond, a, b in (
        (None, partner, strip), (has_from, relay_from, strip), (None, sec, beside), (has_beyond, sec, beyond),
    ):
        when(cond, lambda a=a, b=b: pl.semaphore_signal(barrier, inc=1, device_id=(a, b), device_id_type=MESH))

    loads = [
        pltpu.make_async_copy(src, dst, local_sem.at[i])
        for i, (src, dst) in enumerate((
            (feat.at[0], mine.at[pl.ds(LEFT + STEP, rows)]), (w_one, held_one), (w_two, held_two), (w_three, held_three),
            (b_one, bias_one), (b_two, bias_two), (offsets, moved),
        ))
    ]
    for load in loads:
        load.start()
    pl.semaphore_wait(barrier, 2 + has_to.astype(jnp.int32) + has_beyond.astype(jnp.int32))

    def remote(src, dst, send, recv, a, b):
        return pltpu.make_async_remote_copy(
            src_ref=src, dst_ref=dst, send_sem=send_sem.at[send], recv_sem=recv, device_id=(a, b), device_id_type=MESH
        )

    def top_of(k):
        return jnp.where(core == 0, PAIR * k, rows - PAIR - PAIR * k)

    def direct(k):
        at = top_of(k)
        return remote(feat.at[0, pl.ds(at, PAIR)], wide.at[0, pl.ds(EDGE + at, PAIR)], 0, direct_recv.at[k], partner, strip)

    def relay(k):
        at = pl.ds(EDGE + top_of(k), PAIR)
        return remote(wide.at[0, at], wide.at[1, at], 1, relay_recv.at[k], relay_to, strip)

    def to_beyond(s, k, length):
        at = top_of(k) + core * (PAIR - length)
        to = EDGE + at + rows - 2 * rows * core
        return remote(
            wide.at[s, pl.ds(EDGE + at, length)], wide.at[s, pl.ds(to, length)], 2 + s, beyond_recv.at[s, k], sec, beyond
        )

    def to_beside(s, k, length):
        at = top_of(k) + (1 - core) * (PAIR - length)
        to = EDGE + at - rows + 2 * rows * core
        return remote(
            wide.at[s, pl.ds(EDGE + at, length)], wide.at[s, pl.ds(to, length)], 4 + s, beside_recv.at[s, k - first], sec, beside
        )

    def each_start(k, carry):
        direct(k).start()
        return carry

    lax.fori_loop(0, count, each_start, 0)
    own_low = remote(feat.at[0, pl.ds(0, STEP)], mine.at[pl.ds(LEFT + STEP + rows, STEP)], 6, own_recv.at[0], sec, strip - 1)
    own_high = remote(feat.at[0, pl.ds(rows - STEP, STEP)], mine.at[pl.ds(LEFT, STEP)], 7, own_recv.at[1], sec, strip + 1)
    when(has_low, own_low.start)
    when(has_high, own_high.start)

    zero = jnp.zeros((LEFT,) + mine.shape[1:], mine.dtype)
    mine[0:LEFT] = zero
    mine[LEFT + rows + 2 * STEP:] = zero
    for s in range(2):
        wide[s, 0] = zero[0]
        wide[s, wide.shape[1] - 1] = zero[0]

    @pl.when(jnp.logical_not(has_low))
    def _():
        mine[LEFT:LEFT + STEP] = zero[:STEP]

    @pl.when(jnp.logical_not(has_high))
    def _():
        mine[LEFT + STEP + rows:LEFT + 2 * STEP + rows] = zero[:STEP]

    @pl.when(jnp.logical_not(has_beyond))
    def _():
        for s in range(2):
            wide[s, pl.ds(core * (EDGE + rows), EDGE)] = jnp.zeros((EDGE, cols, chans), wide.dtype)

    scale = chans ** (-0.5)
    lane = lax.broadcasted_iota(jnp.int32, (cols, cols), 1)
    col = lax.broadcasted_iota(jnp.int32, (cols, cols), 0)
    other = col + lax.rem(lane, TAPS) - 4
    inside = (other >= 0) & (other < cols) & (lane < planes)
    source = lane + col - 4
    offset = lane - col + 4

    for load in loads:
        load.wait()
    for d in range(3):
        thirds[8 * d:8 * d + 8] = jnp.zeros((8, hid), thirds.dtype)
        for e in range(3):
            thirds[8 * d + 2 * e:8 * d + 2 * e + 2] = held_three[d, e].astype(thirds.dtype)
    for d in range(2 * 3):
        wide_one[d * cols + planes // 16 * 16:(d + 1) * cols] = jnp.zeros((cols - planes // 16 * 16, 3 * hid), wide_one.dtype)
    for d in range(3):
        for e in range(3):
            at = pl.ds(e * hid, hid)
            for j in range(2):
                wide_one[pl.ds((2 * d + j) * cols, planes), at] = held_one[d, e, j * planes:(j + 1) * planes]
            wide_two[pl.ds(d * hid, hid), at] = held_two[d, e]

    when(has_low, own_high.wait_recv)
    when(has_high, own_low.wait_recv)

    below = jnp.where(sec > 0, -moved[jnp.maximum(sec - 1, 0)], 0)
    above = jnp.where(sec < secs - 1, moved[sec], 0)
    shifts = (jnp.where(odd == 1, below, above), jnp.where(odd == 1, above, below))

    def meet(s, w):
        shift = jnp.where(s == 0, shifts[0], shifts[1])
        turned = [pltpu.roll(wide[s, w + u], lax.rem(TAPS * (w + u), cols), 0) for u in range(QUAD)]
        place = (offset - TAPS * w) & (cols - 1)
        here = mine[pl.ds(w + LEFT - SPAN - 1 - shift, SPAN + PAIR)]
        tiles = []
        for v in range(2):
            own = here[v * PAIR:v * PAIR + SPAN].reshape(SPAN * cols, chans)
            there = jnp.concatenate(turned[v * PAIR:(v + 1) * PAIR], axis=0)
            tiles.append(lax.dot_general(own, there, (((1,), (1,)), ((), ())), preferred_element_type=jnp.float32))
        for j in range(SPAN + PAIR):
            us = [u for u in range(QUAD) if 0 <= TAPS - 1 - j + u < TAPS]
            kept = met[s, w + j]
            found = kept
            for u in reversed(us):
                r = j - u // PAIR * PAIR
                one = tiles[u // PAIR][r * cols:(r + 1) * cols, u % PAIR * cols:(u % PAIR + 1) * cols]
                found = jnp.where(place < TAPS * (u + 1), one, found)
            if us[0] > 0:
                found = jnp.where(place < TAPS * us[0], kept, found)
            met[s, w + j] = found

    def gather(s, at):
        def one(g, carry):
            for i in range(STEP):
                e = g * STEP + i
                start = e + STEP + shifts[s]
                index = (source + TAPS * start) & (cols - 1)
                moved_row = jnp.take_along_axis(
                    met[s, e + SPAN + 1 + shifts[s]], index, axis=1, mode="promise_in_bounds"
                )
                corr[at, e] = jnp.where(inside, moved_row * scale, 0.0).astype(corr.dtype)
            return carry

        lax.fori_loop(0, (rows + 2 * STEP) // STEP, one, 0)

    def halo(s, at):
        k_beyond = (EDGE - PAIR - at) // PAIR
        k_beside = (EDGE + 2 * rows - PAIR - at) // PAIR
        low, high = (at < EDGE) & has_beyond, at >= EDGE + rows
        when(low & (k_beyond < HALO - 1), lambda: to_beyond(s, k_beyond, PAIR).wait_recv())
        when(low & (k_beyond == HALO - 1), lambda: to_beyond(s, k_beyond, PAIR - 1).wait_recv())
        when(high & (k_beside > first), lambda: to_beside(s, k_beside, PAIR).wait_recv())
        when(high & (k_beside == first), lambda: to_beside(s, k_beside, PAIR - 1).wait_recv())

    table = plan(rows)
    stages, width = len(table[0]), len(table)
    codes = [sum(v << (BITS * i) for i, v in enumerate(line)) for line in table]

    def step(n, carry):
        q = lax.rem(n, width)
        m = n // width
        s = lax.rem(m, 2)
        j = m // 2
        k = j - RELAYED * s
        known = (s == 0) | has_from

        @pl.when(known & (q == 0) & (k >= 0) & (k < count))
        def _():
            when(s == 0, lambda: direct(k).wait_recv())
            when(s == 1, lambda: relay(k).wait_recv())
            when((s == 0) & has_to, lambda: relay(k).start())
            when(has_beyond & (k < HALO - 1), lambda: to_beyond(s, k, PAIR).start())
            when(has_beyond & (k == HALO - 1), lambda: to_beyond(s, k, PAIR - 1).start())
            when(k > first, lambda: to_beside(s, k, PAIR).start())
            when(k == first, lambda: to_beside(s, k, PAIR - 1).start())

        code = codes[0]
        for i in range(1, width):
            code = jnp.where(q == i, codes[i], code)
        task = lax.shift_right_logical(jnp.int32(code), BITS * jnp.clip(k, 0, stages - 1)) & (2 ** BITS - 1)

        @pl.when(known & (k >= 0) & (k < stages) & (task > 0))
        def _():
            w = QUAD * (task - 1)
            halo(s, w)
            halo(s, w + PAIR)
            meet(s, jnp.where(core == 0, w, rows + 2 * EDGE - QUAD - w))

        when((s == 0) & (q == 0) & (j == stages), lambda: gather(0, 1 - odd))
        return carry

    lax.fori_loop(0, (stages + RELAYED) * 2 * width, step, 0)

    when(has_from, lambda: gather(1, odd))

    @pl.when(jnp.logical_not(has_from))
    def _():
        corr[odd] = jnp.zeros(corr.shape[1:], corr.dtype)

    convolve((corr.at[0], corr.at[1]), wide_one, bias_one, hid_one)

    @pl.when(strip == 0)
    def _():
        hid_one[0:2] = jnp.zeros((2, cols, hid), hid_one.dtype)

    @pl.when(strip == strips - 1)
    def _():
        hid_one[rows + 2:] = jnp.zeros((2, cols, hid), hid_one.dtype)

    convolve((hid_one,), wide_two, bias_two, hid_two)

    @pl.when(strip == 0)
    def _():
        hid_two[0:1] = jnp.zeros((1, cols, hid), hid_two.dtype)

    @pl.when(strip == strips - 1)
    def _():
        hid_two[rows + 1:] = jnp.zeros((1, cols, hid), hid_two.dtype)

    taps = lax.dot_general(
        thirds[...].astype(hid_two.dtype), hid_two[...].reshape((rows + 2) * cols, hid), (((1,), (1,)), ((), ())),
        preferred_element_type=jnp.float32,
    )
    at_lane = lax.broadcasted_iota(jnp.int32, (8, cols), 1)
    found = []
    for r in range(rows):
        total = sum(taps[8 * d:8 * d + 8, (r + d) * cols:(r + d + 1) * cols] for d in range(3))
        before = jnp.where(at_lane == 0, 0.0, pltpu.roll(total, 1, 1))
        after = jnp.where(at_lane == cols - 1, 0.0, pltpu.roll(total, cols - 1, 1))
        found.append(before[0:2] + total[2:4] + after[4:6])
    turned = jnp.concatenate(found, axis=0)
    for r in range(rows):
        for p in range(2):
            out[p * rows + r] = turned[2 * r + p:2 * r + p + 1]

    def sent(s, length, send, a, b):
        at = pl.ds(EDGE, length)
        return remote(wide.at[s, at], wide.at[s, at], send, direct_recv.at[0], a, b).wait_send

    sent(0, rows, 0, partner, strip)()
    when(has_to, sent(0, rows, 1, relay_to, strip))
    for s, known in ((0, None), (1, has_from)):
        when(both(known, has_beyond), sent(s, SIDE, 2 + s, sec, beyond))
        when(known, sent(s, SIDE, 4 + s, sec, beside))
    when(has_low, own_low.wait_send)
    when(has_high, own_high.wait_send)


def body(secs, strips, features, offsets, state, w_first, b_first, w_second, b_second, w_third):
    _, rows, cols, chans = features.shape
    hid = w_first.shape[3]
    parts = w_third.shape[3]
    bf16 = jnp.bfloat16
    count = rows // PAIR
    thirds = jnp.transpose(w_third, (0, 1, 3, 2))
    dma = pltpu.SemaphoreType.DMA
    delta = pl.pallas_call(
        functools.partial(kernel, secs, strips),
        out_shape=jax.ShapeDtypeStruct((parts * rows, 1, cols), jnp.float32),
        in_specs=[HBM] * 7,
        out_specs=VMEM,
        scratch_shapes=[
            pltpu.VMEM((rows + 2 * STEP + 2 * LEFT, cols, chans), bf16),
            pltpu.VMEM((2, rows + 2 * EDGE, cols, chans), bf16),
            pltpu.VMEM((2, rows + 2 * EDGE + SPAN, cols, cols), jnp.float32),
            pltpu.VMEM((2, rows + 2 * STEP, cols, cols), bf16),
            pltpu.VMEM((rows + 4, cols, hid), bf16),
            pltpu.VMEM((rows + 2, cols, hid), bf16),
            pltpu.VMEM(w_first.shape, bf16),
            pltpu.VMEM(w_second.shape, bf16),
            pltpu.VMEM(thirds.shape, bf16),
            pltpu.VMEM((1, hid), jnp.float32),
            pltpu.VMEM((1, hid), jnp.float32),
            pltpu.SMEM(offsets.shape, jnp.int32),
            pltpu.VMEM((6 * cols, 3 * hid), bf16),
            pltpu.VMEM((3 * hid, 3 * hid), bf16),
            pltpu.VMEM((24, hid), jnp.float32),
            dma((count,)),
            dma((count,)),
            dma((2, HALO)),
            dma((2, HALO)),
            dma((2,)),
            dma((8,)),
            dma((7,)),
        ],
        compiler_params=pltpu.CompilerParams(collective_id=0, has_side_effects=True, vmem_limit_bytes=24 << 20),
    )(*(pltpu.with_memory_space_constraint(x, pltpu.HBM) for x in (features, offsets, w_first, b_first.reshape(1, hid), w_second, b_second.reshape(1, hid), thirds)))
    return state + delta.reshape(state.shape)


def solution(mesh):
    secs, strips = mesh.shape["sec"], mesh.shape["strip"]
    in_specs = (
        P("sec", "strip", None, None),
        P(),
        P(None, "sec", "strip", None),
        P(),
        P(),
        P(),
        P(),
        P(),
    )
    out_specs = P(None, "sec", "strip", None)
    return jax.shard_map(functools.partial(body, secs, strips), mesh=mesh, in_specs=in_specs, out_specs=out_specs, check_vma=False)
```

```python
import functools

import jax
import jax.numpy as jnp
from jax import lax
from jax.experimental import pallas as pl
from jax.experimental.pallas import tpu as pltpu
from jax.sharding import PartitionSpec as P

SIDE = 9
STEP = 3
PAIR = 2
TAPS = 9
SPAN = TAPS + 1
LEFT = SPAN + STEP
EDGE = SIDE + 1
HALO = EDGE // PAIR
QUAD = 2 * PAIR
RELAYED = 2
LATER = 1
SHORT = 7
BITS = 4
HBM = pl.BlockSpec(memory_space=pltpu.HBM)
VMEM = pl.BlockSpec(memory_space=pltpu.VMEM)
MESH = pl.DeviceIdType.MESH


def group_of(rows):
    return max(g for g in range(2, 15, 2) if rows % g == 0)


def when(cond, act):
    if cond is None:
        act()
    else:
        pl.when(cond)(act)


def both(x, y):
    return y if x is None else x & y


def plan(rows):
    count = rows // PAIR
    tasks = {}
    for w in range(0, rows + 2 * EDGE, QUAD):
        ready = []
        for at in (w, w + PAIR):
            if at < EDGE:
                ready.append((EDGE - PAIR - at) // PAIR + 2)
            elif at >= EDGE + rows:
                ready.append((EDGE + 2 * rows - PAIR - at) // PAIR + 1)
            else:
                ready.append((at - EDGE) // PAIR)
        tasks.setdefault(max(ready), []).append(w // QUAD + 1)
    stages = max(max(tasks) + 1, count)
    width = max(len(found) for found in tasks.values())
    return [[(tasks.get(i, []) + [0] * width)[q] for i in range(stages)] for q in range(width)]


def convolve(sources, weight, tail, bias, target, base, group):
    cols, width = target.shape[1:]
    at_col = lax.broadcasted_iota(jnp.int32, (cols, width), 0)

    def taken(rows, depths):
        return jnp.concatenate(
            [jnp.concatenate([s[base + r + d] for r in rows], axis=0) for d in depths for s in sources], axis=1
        )

    main = jnp.dot(taken(range(group), range(3)), weight[...], preferred_element_type=jnp.float32)
    rest = jnp.dot(taken(range(0, group, 2), range(4)), tail[...], preferred_element_type=jnp.float32)
    for i in range(group):
        one = main[i * cols:(i + 1) * cols]
        other = rest[i // 2 * cols:(i // 2 + 1) * cols, i % 2 * width:(i % 2 + 1) * width]
        before = jnp.where(at_col == 0, 0.0, pltpu.roll(one[:, :width], 1, 0))
        after = jnp.where(at_col == cols - 1, 0.0, pltpu.roll(other, cols - 1, 0))
        total = one[:, width:2 * width] + before + after + bias[...]
        target[base + i] = jnp.maximum(total, 0.0).astype(target.dtype)


def kernel(secs, strips, feat, offsets, w_one, b_one, w_two, b_two, w_three, out,
           mine, wide, met, corr, hid_one, hid_two, held_one, held_two, held_three, bias_one, bias_two, moved,
           main_one, rest_one, main_two, rest_two, thirds, direct_recv, relay_recv, beyond_recv, beside_recv, own_recv, send_sem, local_sem):
    rows, cols, chans = feat.shape[1:]
    hid = w_two.shape[3]
    planes = w_one.shape[2] // 2
    count = rows // PAIR
    first = count - HALO
    sec, strip = lax.axis_index("sec"), lax.axis_index("strip")
    odd = lax.rem(sec, 2)
    partner = sec + 1 - 2 * odd
    relay_to, relay_from = sec + 2 - 4 * odd, sec - 2 + 4 * odd
    has_to = (relay_to >= 0) & (relay_to < secs)
    has_from = (relay_from >= 0) & (relay_from < secs)
    has_low, has_high = strip > 0, strip < strips - 1
    core = lax.rem(strip, 2)
    beyond, beside = strip - 1 + 2 * core, strip + 1 - 2 * core
    has_beyond = (beyond >= 0) & (beyond < strips)

    barrier = pltpu.get_barrier_semaphore()
    for cond, a, b in (
        (None, partner, strip), (has_from, relay_from, strip), (None, sec, beside), (has_beyond, sec, beyond),
    ):
        when(cond, lambda a=a, b=b: pl.semaphore_signal(barrier, inc=1, device_id=(a, b), device_id_type=MESH))

    loads = [
        pltpu.make_async_copy(src, dst, local_sem.at[i])
        for i, (src, dst) in enumerate((
            (feat.at[0], mine.at[pl.ds(LEFT + STEP, rows)]), (w_one, held_one), (w_two, held_two), (w_three, held_three),
            (b_one, bias_one), (b_two, bias_two), (offsets, moved),
        ))
    ]
    for load in loads:
        load.start()
    pl.semaphore_wait(barrier, 2 + has_to.astype(jnp.int32) + has_beyond.astype(jnp.int32))

    def remote(src, dst, send, recv, a, b):
        return pltpu.make_async_remote_copy(
            src_ref=src, dst_ref=dst, send_sem=send_sem.at[send], recv_sem=recv, device_id=(a, b), device_id_type=MESH
        )

    def top_of(k):
        return jnp.where(core == 0, PAIR * k, rows - PAIR - PAIR * k)

    def direct(k):
        at = top_of(k)
        return remote(feat.at[0, pl.ds(at, PAIR)], wide.at[0, pl.ds(EDGE + at, PAIR)], 0, direct_recv.at[k], partner, strip)

    def relay(k):
        at = pl.ds(EDGE + top_of(k), PAIR)
        return remote(wide.at[0, at], wide.at[1, at], 1, relay_recv.at[k], relay_to, strip)

    def to_beyond(s, k, length):
        at = top_of(k) + core * (PAIR - length)
        to = EDGE + at + rows - 2 * rows * core
        return remote(
            wide.at[s, pl.ds(EDGE + at, length)], wide.at[s, pl.ds(to, length)], 2 + s, beyond_recv.at[s, k], sec, beyond
        )

    def to_beside(s, k, length):
        at = top_of(k) + (1 - core) * (PAIR - length)
        to = EDGE + at - rows + 2 * rows * core
        return remote(
            wide.at[s, pl.ds(EDGE + at, length)], wide.at[s, pl.ds(to, length)], 4 + s, beside_recv.at[s, k - first], sec, beside
        )

    def each_start(k, carry):
        direct(k).start()
        return carry

    lax.fori_loop(0, count, each_start, 0)
    own_low = remote(feat.at[0, pl.ds(0, STEP)], mine.at[pl.ds(LEFT + STEP + rows, STEP)], 6, own_recv.at[0], sec, strip - 1)
    own_high = remote(feat.at[0, pl.ds(rows - STEP, STEP)], mine.at[pl.ds(LEFT, STEP)], 7, own_recv.at[1], sec, strip + 1)
    when(has_low, own_low.start)
    when(has_high, own_high.start)

    zero = jnp.zeros((LEFT,) + mine.shape[1:], mine.dtype)
    mine[0:LEFT] = zero
    mine[LEFT + rows + 2 * STEP:] = zero
    for s in range(2):
        wide[s, 0] = zero[0]
        wide[s, wide.shape[1] - 1] = zero[0]

    @pl.when(jnp.logical_not(has_low))
    def _():
        mine[LEFT:LEFT + STEP] = zero[:STEP]

    @pl.when(jnp.logical_not(has_high))
    def _():
        mine[LEFT + STEP + rows:LEFT + 2 * STEP + rows] = zero[:STEP]

    @pl.when(jnp.logical_not(has_beyond))
    def _():
        for s in range(2):
            wide[s, pl.ds(core * (EDGE + rows), EDGE)] = jnp.zeros((EDGE, cols, chans), wide.dtype)

    scale = chans ** (-0.5)
    lane = lax.broadcasted_iota(jnp.int32, (cols, cols), 1)
    col = lax.broadcasted_iota(jnp.int32, (cols, cols), 0)
    other = col + lax.rem(lane, TAPS) - 4
    inside = (other >= 0) & (other < cols) & (lane < planes)
    source = lane + col - 4
    offset = lane - col + 4

    for load in loads:
        load.wait()
    for d in range(3):
        thirds[8 * d:8 * d + 8] = jnp.zeros((8, hid), thirds.dtype)
        for e in range(3):
            thirds[8 * d + 2 * e:8 * d + 2 * e + 2] = held_three[d, e].astype(thirds.dtype)
    for ref in (main_one, rest_one, rest_two):
        ref[...] = jnp.zeros(ref.shape, ref.dtype)
    for d in range(3):
        for j, place in ((0, 1 - odd), (1, odd)):
            part = pl.ds(j * planes, planes)
            at = pl.ds(pl.multiple_of((2 * d + place) * cols, cols), planes)
            next_at = pl.ds(pl.multiple_of((2 * d + 2 + place) * cols, cols), planes)
            for e in range(2):
                main_one[at, e * hid:(e + 1) * hid] = held_one[d, e, part]
            rest_one[at, 0:hid] = held_one[d, 2, part]
            rest_one[next_at, hid:2 * hid] = held_one[d, 2, part]
        at, next_at = pl.ds(d * hid, hid), pl.ds((d + 1) * hid, hid)
        for e in range(2):
            main_two[at, e * hid:(e + 1) * hid] = held_two[d, e]
        rest_two[at, 0:hid] = held_two[d, 2]
        rest_two[next_at, hid:2 * hid] = held_two[d, 2]

    when(has_low, own_high.wait_recv)
    when(has_high, own_low.wait_recv)

    below = jnp.where(sec > 0, -moved[jnp.maximum(sec - 1, 0)], 0)
    above = jnp.where(sec < secs - 1, moved[sec], 0)
    shifts = (jnp.where(odd == 1, below, above), jnp.where(odd == 1, above, below))

    def turned(s, w):
        return [pltpu.roll(wide[s, w + u], (TAPS * (w + u)) & (cols - 1), 0) for u in range(QUAD)]

    def product(own, there):
        return lax.dot_general(
            own.reshape(-1, chans), jnp.concatenate(there, axis=0), (((1,), (1,)), ((), ())),
            preferred_element_type=jnp.float32,
        )

    def shift_of(s):
        return jnp.where(s == 0, shifts[0], shifts[1])

    def meet(s, w):
        there = turned(s, w)
        place = (offset - TAPS * w) & (cols - 1)
        here = mine[pl.ds(w + LEFT - SPAN - 1 - shift_of(s), SPAN + PAIR)]
        tiles = [product(here[v * PAIR:v * PAIR + SPAN], there[v * PAIR:(v + 1) * PAIR]) for v in range(2)]
        for j in range(SPAN + PAIR):
            us = [u for u in range(QUAD) if 0 <= TAPS - 1 - j + u < TAPS]
            kept = met[s, w + j]
            found = kept
            for u in reversed(us):
                r = j - u // PAIR * PAIR
                one = tiles[u // PAIR][r * cols:(r + 1) * cols, u % PAIR * cols:(u % PAIR + 1) * cols]
                found = jnp.where(place < TAPS * (u + 1), one, found)
            if us[0] > 0:
                found = jnp.where(place < TAPS * us[0], kept, found)
            met[s, w + j] = found

    def meet_edge(s, w):
        there = turned(s, w)
        place = (offset - TAPS * w) & (cols - 1)
        begin = jnp.where(w <= QUAD, SPAN + PAIR - SHORT, 0)
        here = mine[pl.ds(w + begin + LEFT - SPAN - 1 - shift_of(s), SHORT)]
        tiles = [product(here, there[v * PAIR:(v + 1) * PAIR]) for v in range(2)]
        for r in range(SHORT):
            j = begin + r
            low, high = TAPS * jnp.maximum(j - TAPS + 1, 0), TAPS * jnp.minimum(j + 1, QUAD)
            kept = met[s, w + j]
            found = tiles[1][r * cols:(r + 1) * cols, cols:]
            for u in reversed(range(QUAD - 1)):
                one = tiles[u // PAIR][r * cols:(r + 1) * cols, u % PAIR * cols:(u % PAIR + 1) * cols]
                found = jnp.where(place < TAPS * (u + 1), one, found)
            met[s, w + j] = jnp.where((place >= low) & (place < high), found, kept)

    def gather(s, e):
        index = (source + TAPS * (e + STEP + shifts[s])) & (cols - 1)
        moved_row = jnp.take_along_axis(met[s, e + SPAN + 1 + shifts[s]], index, axis=1, mode="promise_in_bounds")
        keep = inside if s == 0 else inside & has_from
        corr[s, e] = jnp.where(keep, moved_row * scale, 0.0).astype(corr.dtype)

    def gather_some(s, start, end):
        def some(g, carry):
            for i in range(PAIR):
                gather(s, start + g * PAIR + i)
            return carry

        lax.fori_loop(0, (end - start) // PAIR, some, 0)

    def halo(s, at):
        k_beyond = (EDGE - PAIR - at) // PAIR
        k_beside = (EDGE + 2 * rows - PAIR - at) // PAIR
        low, high = (at < EDGE) & has_beyond, at >= EDGE + rows
        when(low & (k_beyond < HALO - 1), lambda: to_beyond(s, k_beyond, PAIR).wait_recv())
        when(low & (k_beyond == HALO - 1), lambda: to_beyond(s, k_beyond, PAIR - 1).wait_recv())
        when(high & (k_beside > first), lambda: to_beside(s, k_beside, PAIR).wait_recv())
        when(high & (k_beside == first), lambda: to_beside(s, k_beside, PAIR - 1).wait_recv())

    table = plan(rows)
    stages, width = len(table[0]), len(table)
    codes = [sum(v << (BITS * i) for i, v in enumerate(line)) for line in table]

    def step(n, carry):
        s, j = lax.rem(n, 2), n // 2
        k = j - RELAYED * s
        known = (s == 0) | has_from

        @pl.when(known & (k >= 0) & (k < count))
        def _():
            when(s == 0, lambda: direct(k).wait_recv())
            when(s == 1, lambda: relay(k).wait_recv())
            when((s == 0) & has_to, lambda: relay(k).start())
            when(has_beyond & (k < HALO - 1), lambda: to_beyond(s, k, PAIR).start())
            when(has_beyond & (k == HALO - 1), lambda: to_beyond(s, k, PAIR - 1).start())
            when(k > first, lambda: to_beside(s, k, PAIR).start())
            when(k == first, lambda: to_beside(s, k, PAIR - 1).start())

        t = k - LATER * s

        @pl.when(known & (t >= 0) & (t < stages))
        def _():
            tasks = [lax.shift_right_logical(jnp.int32(code), BITS * t) & (2 ** BITS - 1) for code in codes]

            def work(q, carry):
                task = tasks[0]
                for i in range(1, width):
                    task = jnp.where(q == i, tasks[i], task)
                w = QUAD * (task - 1)
                halo(s, w)
                halo(s, w + PAIR)
                edge = (w <= QUAD) | (w >= rows + EDGE + PAIR)
                at = jnp.where(core == 0, w, rows + 2 * EDGE - QUAD - w)
                when(edge, lambda: meet_edge(s, at))
                when(jnp.logical_not(edge), lambda: meet(s, at))
                return carry

            lax.fori_loop(0, sum((task > 0).astype(jnp.int32) for task in tasks), work, 0)

        when((s == 0) & (j == stages + 1), lambda: gather_some(0, 0, rows + 2 * STEP))
        return carry

    lax.fori_loop(0, (stages + RELAYED + LATER) * 2, step, 0)

    group = group_of(rows + 4)
    gather_some(1, 0, group + PAIR)
    for base in range(0, rows + 4, group):
        for e in range(base + group + PAIR, min(base + 2 * group + PAIR, rows + 2 * STEP)):
            gather(1, e)
        convolve((corr.at[0], corr.at[1]), main_one, rest_one, bias_one, hid_one, base, group)

    @pl.when(strip == 0)
    def _():
        hid_one[0:2] = jnp.zeros((2, cols, hid), hid_one.dtype)

    @pl.when(strip == strips - 1)
    def _():
        hid_one[rows + 2:] = jnp.zeros((2, cols, hid), hid_one.dtype)

    group = group_of(rows + 2)
    for base in range(0, rows + 2, group):
        convolve((hid_one,), main_two, rest_two, bias_two, hid_two, base, group)

    @pl.when(strip == 0)
    def _():
        hid_two[0:1] = jnp.zeros((1, cols, hid), hid_two.dtype)

    @pl.when(strip == strips - 1)
    def _():
        hid_two[rows + 1:] = jnp.zeros((1, cols, hid), hid_two.dtype)

    taps = lax.dot_general(
        thirds[...].astype(hid_two.dtype), hid_two[...].reshape((rows + 2) * cols, hid), (((1,), (1,)), ((), ())),
        preferred_element_type=jnp.float32,
    )
    at_lane = lax.broadcasted_iota(jnp.int32, (8, cols), 1)
    found = []
    for r in range(rows):
        total = sum(taps[8 * d:8 * d + 8, (r + d) * cols:(r + d + 1) * cols] for d in range(3))
        before = jnp.where(at_lane == 0, 0.0, pltpu.roll(total, 1, 1))
        after = jnp.where(at_lane == cols - 1, 0.0, pltpu.roll(total, cols - 1, 1))
        found.append(before[0:2] + total[2:4] + after[4:6])
    turned = jnp.concatenate(found, axis=0)
    for r in range(rows):
        for p in range(2):
            out[p * rows + r] = turned[2 * r + p:2 * r + p + 1]

    def sent(s, length, send, a, b):
        at = pl.ds(EDGE, length)
        return remote(wide.at[s, at], wide.at[s, at], send, direct_recv.at[0], a, b).wait_send

    sent(0, rows, 0, partner, strip)()
    when(has_to, sent(0, rows, 1, relay_to, strip))
    for s, known in ((0, None), (1, has_from)):
        when(both(known, has_beyond), sent(s, SIDE, 2 + s, sec, beyond))
        when(known, sent(s, SIDE, 4 + s, sec, beside))
    when(has_low, own_low.wait_send)
    when(has_high, own_high.wait_send)


def body(secs, strips, features, offsets, state, w_first, b_first, w_second, b_second, w_third):
    _, rows, cols, chans = features.shape
    hid = w_first.shape[3]
    parts = w_third.shape[3]
    bf16 = jnp.bfloat16
    count = rows // PAIR
    thirds = jnp.transpose(w_third, (0, 1, 3, 2))
    dma = pltpu.SemaphoreType.DMA
    delta = pl.pallas_call(
        functools.partial(kernel, secs, strips),
        out_shape=jax.ShapeDtypeStruct((parts * rows, 1, cols), jnp.float32),
        in_specs=[HBM] * 7,
        out_specs=VMEM,
        scratch_shapes=[
            pltpu.VMEM((rows + 2 * STEP + 2 * LEFT, cols, chans), bf16),
            pltpu.VMEM((2, rows + 2 * EDGE, cols, chans), bf16),
            pltpu.VMEM((2, rows + 2 * EDGE + SPAN, cols, cols), jnp.float32),
            pltpu.VMEM((2, rows + 2 * STEP, cols, cols), bf16),
            pltpu.VMEM((rows + 4, cols, hid), bf16),
            pltpu.VMEM((rows + 2, cols, hid), bf16),
            pltpu.VMEM(w_first.shape, bf16),
            pltpu.VMEM(w_second.shape, bf16),
            pltpu.VMEM(thirds.shape, bf16),
            pltpu.VMEM((1, hid), jnp.float32),
            pltpu.VMEM((1, hid), jnp.float32),
            pltpu.SMEM(offsets.shape, jnp.int32),
            pltpu.VMEM((6 * cols, 2 * hid), bf16),
            pltpu.VMEM((8 * cols, 2 * hid), bf16),
            pltpu.VMEM((3 * hid, 2 * hid), bf16),
            pltpu.VMEM((4 * hid, 2 * hid), bf16),
            pltpu.VMEM((24, hid), jnp.float32),
            dma((count,)),
            dma((count,)),
            dma((2, HALO)),
            dma((2, HALO)),
            dma((2,)),
            dma((8,)),
            dma((7,)),
        ],
        compiler_params=pltpu.CompilerParams(collective_id=0, has_side_effects=True, vmem_limit_bytes=24 << 20),
    )(*(pltpu.with_memory_space_constraint(x, pltpu.HBM) for x in (features, offsets, w_first, b_first.reshape(1, hid), w_second, b_second.reshape(1, hid), thirds)))
    return state + delta.reshape(state.shape)


def solution(mesh):
    secs, strips = mesh.shape["sec"], mesh.shape["strip"]
    in_specs = (
        P("sec", "strip", None, None),
        P(),
        P(None, "sec", "strip", None),
        P(),
        P(),
        P(),
        P(),
        P(),
    )
    out_specs = P(None, "sec", "strip", None)
    return jax.shard_map(functools.partial(body, secs, strips), mesh=mesh, in_specs=in_specs, out_specs=out_specs, check_vma=False)
```

```python
import functools

import jax
import jax.numpy as jnp
from jax import lax
from jax.experimental import pallas as pl
from jax.experimental.pallas import tpu as pltpu
from jax.sharding import PartitionSpec as P

SIDE = 9
STEP = 3
PAIR = 2
TAPS = 9
SPAN = TAPS + 1
LEFT = SPAN + STEP
EDGE = SIDE + 1
HALO = EDGE // PAIR
QUAD = 2 * PAIR
RELAYED = 2
LATER = 1
SHORT = 7
BITS = 4
HBM = pl.BlockSpec(memory_space=pltpu.HBM)
VMEM = pl.BlockSpec(memory_space=pltpu.VMEM)
MESH = pl.DeviceIdType.MESH


def group_of(rows):
    return max(g for g in range(2, 15, 2) if rows % g == 0)


def when(cond, act):
    if cond is None:
        act()
    else:
        pl.when(cond)(act)


def both(x, y):
    return y if x is None else x & y


def plan(rows):
    count = rows // PAIR
    tasks = {}
    for w in range(0, rows + 2 * EDGE, QUAD):
        ready = []
        for at in (w, w + PAIR):
            if at < EDGE:
                ready.append((EDGE - PAIR - at) // PAIR + 2)
            elif at >= EDGE + rows:
                ready.append((EDGE + 2 * rows - PAIR - at) // PAIR + 1)
            else:
                ready.append((at - EDGE) // PAIR)
        tasks.setdefault(max(ready), []).append(w // QUAD + 1)
    stages = max(max(tasks) + 1, count)
    width = 2
    for found in tasks.values():
        found.sort(key=lambda task: min(task - 1, (rows + 2 * EDGE) // QUAD - task))
    spill = max(len(found) for found in tasks.values())
    assert spill <= width and rows % QUAD == 0
    return [[(tasks.get(i, []) + [0] * width)[q] for i in range(stages)] for q in range(width)]


def convolve(sources, weight, tail, bias, target, base, group):
    cols, width = target.shape[1:]
    at_col = lax.broadcasted_iota(jnp.int32, (cols, width), 0)

    def taken(rows, depths):
        return jnp.concatenate(
            [jnp.concatenate([s[base + r + d] for r in rows], axis=0) for d in depths for s in sources], axis=1
        )

    main = jnp.dot(taken(range(group), range(3)), weight[...], preferred_element_type=jnp.float32)
    rest = jnp.dot(taken(range(0, group, 2), range(4)), tail[...], preferred_element_type=jnp.float32)
    for i in range(group):
        one = main[i * cols:(i + 1) * cols]
        other = rest[i // 2 * cols:(i // 2 + 1) * cols, i % 2 * width:(i % 2 + 1) * width]
        before = jnp.where(at_col == 0, 0.0, pltpu.roll(one[:, :width], 1, 0))
        after = jnp.where(at_col == cols - 1, 0.0, pltpu.roll(other, cols - 1, 0))
        total = one[:, width:2 * width] + before + after + bias[...]
        target[base + i] = jnp.maximum(total, 0.0).astype(target.dtype)


def kernel(secs, strips, feat, offsets, w_one, b_one, w_two, b_two, w_three, out,
           mine, wide, met, corr, hid_one, hid_two, held_one, held_two, held_three, bias_one, bias_two, moved,
           main_one, rest_one, main_two, rest_two, thirds, direct_recv, relay_recv, beyond_recv, beside_recv, own_recv, send_sem, local_sem):
    rows, cols, chans = feat.shape[1:]
    hid = w_two.shape[3]
    planes = w_one.shape[2] // 2
    count = rows // PAIR
    first = count - HALO
    sec, strip = lax.axis_index("sec"), lax.axis_index("strip")
    odd = lax.rem(sec, 2)
    partner = sec + 1 - 2 * odd
    relay_to, relay_from = sec + 2 - 4 * odd, sec - 2 + 4 * odd
    has_to = (relay_to >= 0) & (relay_to < secs)
    has_from = (relay_from >= 0) & (relay_from < secs)
    has_low, has_high = strip > 0, strip < strips - 1
    core = lax.rem(strip, 2)
    beyond, beside = strip - 1 + 2 * core, strip + 1 - 2 * core
    has_beyond = (beyond >= 0) & (beyond < strips)

    barrier = pltpu.get_barrier_semaphore()
    for cond, a, b in (
        (None, partner, strip), (has_from, relay_from, strip), (None, sec, beside), (has_beyond, sec, beyond),
    ):
        when(cond, lambda a=a, b=b: pl.semaphore_signal(barrier, inc=1, device_id=(a, b), device_id_type=MESH))

    loads = [
        pltpu.make_async_copy(src, dst, local_sem.at[i])
        for i, (src, dst) in enumerate((
            (feat.at[0], mine.at[pl.ds(LEFT + STEP, rows)]), (w_one, held_one), (w_two, held_two), (w_three, held_three),
            (b_one, bias_one), (b_two, bias_two), (offsets, moved),
        ))
    ]
    for load in loads:
        load.start()
    pl.semaphore_wait(barrier, 2 + has_to.astype(jnp.int32) + has_beyond.astype(jnp.int32))

    def remote(src, dst, send, recv, a, b):
        return pltpu.make_async_remote_copy(
            src_ref=src, dst_ref=dst, send_sem=send_sem.at[send], recv_sem=recv, device_id=(a, b), device_id_type=MESH
        )

    def top_of(k):
        return jnp.where(core == 0, PAIR * k, rows - PAIR - PAIR * k)

    def direct(k):
        at = top_of(k)
        return remote(feat.at[0, pl.ds(at, PAIR)], wide.at[0, pl.ds(EDGE + at, PAIR)], 0, direct_recv.at[k], partner, strip)

    def relay(k):
        at = pl.ds(EDGE + top_of(k), PAIR)
        return remote(wide.at[0, at], wide.at[1, at], 1, relay_recv.at[k], relay_to, strip)

    def to_beyond(s, k, length):
        at = top_of(k) + core * (PAIR - length)
        to = EDGE + at + rows - 2 * rows * core
        return remote(
            wide.at[s, pl.ds(EDGE + at, length)], wide.at[s, pl.ds(to, length)], 2 + s, beyond_recv.at[s, k], sec, beyond
        )

    def to_beside(s, k, length):
        at = top_of(k) + (1 - core) * (PAIR - length)
        to = EDGE + at - rows + 2 * rows * core
        return remote(
            wide.at[s, pl.ds(EDGE + at, length)], wide.at[s, pl.ds(to, length)], 4 + s, beside_recv.at[s, k - first], sec, beside
        )

    def each_start(k, carry):
        direct(k).start()
        return carry

    lax.fori_loop(0, count, each_start, 0)
    own_low = remote(feat.at[0, pl.ds(0, STEP)], mine.at[pl.ds(LEFT + STEP + rows, STEP)], 6, own_recv.at[0], sec, strip - 1)
    own_high = remote(feat.at[0, pl.ds(rows - STEP, STEP)], mine.at[pl.ds(LEFT, STEP)], 7, own_recv.at[1], sec, strip + 1)
    when(has_low, own_low.start)
    when(has_high, own_high.start)

    zero = jnp.zeros((LEFT,) + mine.shape[1:], mine.dtype)
    mine[0:LEFT] = zero
    mine[LEFT + rows + 2 * STEP:] = zero
    for s in range(2):
        wide[s, 0] = zero[0]
        wide[s, wide.shape[1] - 1] = zero[0]

    @pl.when(jnp.logical_not(has_low))
    def _():
        mine[LEFT:LEFT + STEP] = zero[:STEP]

    @pl.when(jnp.logical_not(has_high))
    def _():
        mine[LEFT + STEP + rows:LEFT + 2 * STEP + rows] = zero[:STEP]

    @pl.when(jnp.logical_not(has_beyond))
    def _():
        for s in range(2):
            wide[s, pl.ds(core * (EDGE + rows), EDGE)] = jnp.zeros((EDGE, cols, chans), wide.dtype)

    scale = chans ** (-0.5)
    lane = lax.broadcasted_iota(jnp.int32, (cols, cols), 1)
    col = lax.broadcasted_iota(jnp.int32, (cols, cols), 0)
    other = col + lax.rem(lane, TAPS) - 4
    inside = (other >= 0) & (other < cols) & (lane < planes)
    source = lane + col - 4
    offset = lane - col + 4

    for load in loads:
        load.wait()
    for d in range(3):
        thirds[8 * d:8 * d + 8] = jnp.zeros((8, hid), thirds.dtype)
        for e in range(3):
            thirds[8 * d + 2 * e:8 * d + 2 * e + 2] = held_three[d, e].astype(thirds.dtype)
    for ref in (main_one, rest_one, rest_two):
        ref[...] = jnp.zeros(ref.shape, ref.dtype)
    for d in range(3):
        for j, place in ((0, 1 - odd), (1, odd)):
            part = pl.ds(j * planes, planes)
            at = pl.ds(pl.multiple_of((2 * d + place) * cols, cols), planes)
            next_at = pl.ds(pl.multiple_of((2 * d + 2 + place) * cols, cols), planes)
            for e in range(2):
                main_one[at, e * hid:(e + 1) * hid] = held_one[d, e, part]
            rest_one[at, 0:hid] = held_one[d, 2, part]
            rest_one[next_at, hid:2 * hid] = held_one[d, 2, part]
        at, next_at = pl.ds(d * hid, hid), pl.ds((d + 1) * hid, hid)
        for e in range(2):
            main_two[at, e * hid:(e + 1) * hid] = held_two[d, e]
        rest_two[at, 0:hid] = held_two[d, 2]
        rest_two[next_at, hid:2 * hid] = held_two[d, 2]

    when(has_low, own_high.wait_recv)
    when(has_high, own_low.wait_recv)

    below = jnp.where(sec > 0, -moved[jnp.maximum(sec - 1, 0)], 0)
    above = jnp.where(sec < secs - 1, moved[sec], 0)
    shifts = (jnp.where(odd == 1, below, above), jnp.where(odd == 1, above, below))

    def turned(s, w):
        return [pltpu.roll(wide[s, w + u], (TAPS * (w + u)) & (cols - 1), 0) for u in range(QUAD)]

    def product(own, there):
        return lax.dot_general(
            own.reshape(-1, chans), jnp.concatenate(there, axis=0), (((1,), (1,)), ((), ())),
            preferred_element_type=jnp.float32,
        )

    def shift_of(s):
        return jnp.where(s == 0, shifts[0], shifts[1])

    def full(s, w):
        there = turned(s, w)
        here = mine[pl.ds(w + LEFT - SPAN - 1 - shift_of(s), SPAN + PAIR)]
        tiles = [product(here[v * PAIR:v * PAIR + SPAN], there[v * PAIR:(v + 1) * PAIR]) for v in range(2)]

        def keep():
            place = (offset - TAPS * w) & (cols - 1)
            for j in range(SPAN + PAIR):
                us = [u for u in range(QUAD) if 0 <= TAPS - 1 - j + u < TAPS]
                kept = met[s, w + j]
                found = kept
                for u in reversed(us):
                    r = j - u // PAIR * PAIR
                    one = tiles[u // PAIR][r * cols:(r + 1) * cols, u % PAIR * cols:(u % PAIR + 1) * cols]
                    found = jnp.where(place < TAPS * (u + 1), one, found)
                if us[0] > 0:
                    found = jnp.where(place < TAPS * us[0], kept, found)
                met[s, w + j] = found

        return keep

    def edge(s, w):
        there = turned(s, w)
        begin = jnp.where(w <= QUAD, SPAN + PAIR - SHORT, 0)
        here = mine[pl.ds(w + begin + LEFT - SPAN - 1 - shift_of(s), SHORT)]
        tiles = [product(here, there[v * PAIR:(v + 1) * PAIR]) for v in range(2)]

        def keep():
            place = (offset - TAPS * w) & (cols - 1)
            for r in range(SHORT):
                j = begin + r
                low, high = TAPS * jnp.maximum(j - TAPS + 1, 0), TAPS * jnp.minimum(j + 1, QUAD)
                kept = met[s, w + j]
                found = tiles[1][r * cols:(r + 1) * cols, cols:]
                for u in reversed(range(QUAD - 1)):
                    one = tiles[u // PAIR][r * cols:(r + 1) * cols, u % PAIR * cols:(u % PAIR + 1) * cols]
                    found = jnp.where(place < TAPS * (u + 1), one, found)
                met[s, w + j] = jnp.where((place >= low) & (place < high), found, kept)

        return keep

    def meet(*steps):
        for keep in [act(s, w) for act, s, w in steps]:
            keep()

    def gather(s, e):
        index = (source + TAPS * (e + STEP + shifts[s])) & (cols - 1)
        moved_row = jnp.take_along_axis(met[s, e + SPAN + 1 + shifts[s]], index, axis=1, mode="promise_in_bounds")
        keep = inside if s == 0 else inside & has_from
        corr[s, e] = jnp.where(keep, moved_row * scale, 0.0).astype(corr.dtype)

    def gather_some(s, start, end):
        def some(g, carry):
            for i in range(6):
                gather(s, start + g * 6 + i)
            return carry

        lax.fori_loop(0, (end - start) // 6, some, 0)

    def halo(s, at):
        k_beyond = (EDGE - PAIR - at) // PAIR
        k_beside = (EDGE + 2 * rows - PAIR - at) // PAIR
        low, high = (at < EDGE) & has_beyond, at >= EDGE + rows
        when(low & (k_beyond < HALO - 1), lambda: to_beyond(s, k_beyond, PAIR).wait_recv())
        when(low & (k_beyond == HALO - 1), lambda: to_beyond(s, k_beyond, PAIR - 1).wait_recv())
        when(high & (k_beside > first), lambda: to_beside(s, k_beside, PAIR).wait_recv())
        when(high & (k_beside == first), lambda: to_beside(s, k_beside, PAIR - 1).wait_recv())

    table = plan(rows)
    stages, width = len(table[0]), len(table)
    lone_full = any(QUAD < QUAD * (a - 1) < rows + EDGE + PAIR for a, b in zip(*table) if a > 0 and b == 0)
    codes = [sum(v << (BITS * i) for i, v in enumerate(line)) for line in table]

    def step(n, carry):
        s, j = lax.rem(n, 2), n // 2
        k = j - RELAYED * s
        known = (s == 0) | has_from

        @pl.when(known & (k >= 0) & (k < count))
        def _():
            when(s == 0, lambda: direct(k).wait_recv())
            when(s == 1, lambda: relay(k).wait_recv())
            when((s == 0) & has_to, lambda: relay(k).start())
            when(has_beyond & (k < HALO - 1), lambda: to_beyond(s, k, PAIR).start())
            when(has_beyond & (k == HALO - 1), lambda: to_beyond(s, k, PAIR - 1).start())
            when(k > first, lambda: to_beside(s, k, PAIR).start())
            when(k == first, lambda: to_beside(s, k, PAIR - 1).start())

        t = k - LATER * s

        @pl.when(known & (t >= 0) & (t < stages))
        def _():
            tasks = [lax.shift_right_logical(jnp.int32(code), BITS * t) & (2 ** BITS - 1) for code in codes]

            ws = [QUAD * (task - 1) for task in tasks]
            ats = [jnp.where(core == 0, w, rows + 2 * EDGE - QUAD - w) for w in ws]
            short = [(w <= QUAD) | (w >= rows + EDGE + PAIR) for w in ws]
            has_two = tasks[1] > 0

            @pl.when(tasks[0] > 0)
            def _():
                halo(s, ws[0])
                halo(s, ws[0] + PAIR)

            @pl.when(has_two)
            def _():
                halo(s, ws[1])
                halo(s, ws[1] + PAIR)

            alone = (tasks[0] > 0) & jnp.logical_not(has_two)
            when(alone & short[0], lambda: meet((edge, s, ats[0])))
            if lone_full:
                when(alone & jnp.logical_not(short[0]), lambda: meet((full, s, ats[0])))
            when(has_two & short[0], lambda: meet((edge, s, ats[0]), (full, s, ats[1])))
            when(has_two & jnp.logical_not(short[0]), lambda: meet((full, s, ats[0]), (full, s, ats[1])))

        when((s == 0) & (j == stages + 1), lambda: gather_some(0, 0, rows + 2 * STEP))
        return carry

    lax.fori_loop(0, (stages + RELAYED + LATER) * 2, step, 0)

    group = group_of(rows + 4)
    ready = pl.cdiv(group + PAIR, 6) * 6
    gather_some(1, 0, ready)
    for base in range(0, rows + 4, group):
        for e in range(max(base + group + PAIR, ready), min(base + 2 * group + PAIR, rows + 2 * STEP)):
            gather(1, e)
        convolve((corr.at[0], corr.at[1]), main_one, rest_one, bias_one, hid_one, base, group)

    @pl.when(strip == 0)
    def _():
        hid_one[0:2] = jnp.zeros((2, cols, hid), hid_one.dtype)

    @pl.when(strip == strips - 1)
    def _():
        hid_one[rows + 2:] = jnp.zeros((2, cols, hid), hid_one.dtype)

    group = group_of(rows + 2)
    for base in range(0, rows + 2, group):
        convolve((hid_one,), main_two, rest_two, bias_two, hid_two, base, group)

    @pl.when(strip == 0)
    def _():
        hid_two[0:1] = jnp.zeros((1, cols, hid), hid_two.dtype)

    @pl.when(strip == strips - 1)
    def _():
        hid_two[rows + 1:] = jnp.zeros((1, cols, hid), hid_two.dtype)

    taps = lax.dot_general(
        thirds[...].astype(hid_two.dtype), hid_two[...].reshape((rows + 2) * cols, hid), (((1,), (1,)), ((), ())),
        preferred_element_type=jnp.float32,
    )
    at_lane = lax.broadcasted_iota(jnp.int32, (8, cols), 1)
    found = []
    for r in range(rows):
        total = sum(taps[8 * d:8 * d + 8, (r + d) * cols:(r + d + 1) * cols] for d in range(3))
        before = jnp.where(at_lane == 0, 0.0, pltpu.roll(total, 1, 1))
        after = jnp.where(at_lane == cols - 1, 0.0, pltpu.roll(total, cols - 1, 1))
        found.append(before[0:2] + total[2:4] + after[4:6])
    turned = jnp.concatenate(found, axis=0)
    for r in range(rows):
        for p in range(2):
            out[p * rows + r] = turned[2 * r + p:2 * r + p + 1]

    def sent(s, length, send, a, b):
        at = pl.ds(EDGE, length)
        return remote(wide.at[s, at], wide.at[s, at], send, direct_recv.at[0], a, b).wait_send

    sent(0, rows, 0, partner, strip)()
    when(has_to, sent(0, rows, 1, relay_to, strip))
    for s, known in ((0, None), (1, has_from)):
        when(both(known, has_beyond), sent(s, SIDE, 2 + s, sec, beyond))
        when(known, sent(s, SIDE, 4 + s, sec, beside))
    when(has_low, own_low.wait_send)
    when(has_high, own_high.wait_send)


def body(secs, strips, features, offsets, state, w_first, b_first, w_second, b_second, w_third):
    _, rows, cols, chans = features.shape
    hid = w_first.shape[3]
    parts = w_third.shape[3]
    bf16 = jnp.bfloat16
    count = rows // PAIR
    thirds = jnp.transpose(w_third, (0, 1, 3, 2))
    dma = pltpu.SemaphoreType.DMA
    delta = pl.pallas_call(
        functools.partial(kernel, secs, strips),
        out_shape=jax.ShapeDtypeStruct((parts * rows, 1, cols), jnp.float32),
        in_specs=[HBM] * 7,
        out_specs=VMEM,
        scratch_shapes=[
            pltpu.VMEM((rows + 2 * STEP + 2 * LEFT, cols, chans), bf16),
            pltpu.VMEM((2, rows + 2 * EDGE, cols, chans), bf16),
            pltpu.VMEM((2, rows + 2 * EDGE + SPAN, cols, cols), jnp.float32),
            pltpu.VMEM((2, rows + 2 * STEP, cols, cols), bf16),
            pltpu.VMEM((rows + 4, cols, hid), bf16),
            pltpu.VMEM((rows + 2, cols, hid), bf16),
            pltpu.VMEM(w_first.shape, bf16),
            pltpu.VMEM(w_second.shape, bf16),
            pltpu.VMEM(thirds.shape, bf16),
            pltpu.VMEM((1, hid), jnp.float32),
            pltpu.VMEM((1, hid), jnp.float32),
            pltpu.SMEM(offsets.shape, jnp.int32),
            pltpu.VMEM((6 * cols, 2 * hid), bf16),
            pltpu.VMEM((8 * cols, 2 * hid), bf16),
            pltpu.VMEM((3 * hid, 2 * hid), bf16),
            pltpu.VMEM((4 * hid, 2 * hid), bf16),
            pltpu.VMEM((24, hid), jnp.float32),
            dma((count,)),
            dma((count,)),
            dma((2, HALO)),
            dma((2, HALO)),
            dma((2,)),
            dma((8,)),
            dma((7,)),
        ],
        compiler_params=pltpu.CompilerParams(collective_id=0, has_side_effects=True, vmem_limit_bytes=24 << 20),
    )(*(pltpu.with_memory_space_constraint(x, pltpu.HBM) for x in (features, offsets, w_first, b_first.reshape(1, hid), w_second, b_second.reshape(1, hid), thirds)))
    return state + delta.reshape(state.shape)


def solution(mesh):
    secs, strips = mesh.shape["sec"], mesh.shape["strip"]
    in_specs = (
        P("sec", "strip", None, None),
        P(),
        P(None, "sec", "strip", None),
        P(),
        P(),
        P(),
        P(),
        P(),
    )
    out_specs = P(None, "sec", "strip", None)
    return jax.shard_map(functools.partial(body, secs, strips), mesh=mesh, in_specs=in_specs, out_specs=out_specs, check_vma=False)
```

```python
import functools

import jax
import jax.numpy as jnp
from jax import lax
from jax.experimental import pallas as pl
from jax.experimental.pallas import tpu as pltpu
from jax.sharding import PartitionSpec as P

SIDE = 9
STEP = 3
PAIR = 2
TAPS = 9
SPAN = TAPS + 1
LEFT = SPAN + STEP
EDGE = SIDE + 1
HALO = EDGE // PAIR
QUAD = 2 * PAIR
RELAYED = 3
LATER = 0
SHORT = 7
BLOCK = 6
BITS = 4
HBM = pl.BlockSpec(memory_space=pltpu.HBM)
VMEM = pl.BlockSpec(memory_space=pltpu.VMEM)
MESH = pl.DeviceIdType.MESH


def group_of(rows, most):
    return max(g for g in range(2, most + 1, 2) if rows % g == 0)


def when(cond, act):
    if cond is None:
        act()
    else:
        pl.when(cond)(act)


def both(x, y):
    return y if x is None else x & y


def plan(rows):
    count = rows // PAIR
    tasks = {}
    for w in range(0, rows + 2 * EDGE, QUAD):
        ready = []
        for at in (w, w + PAIR):
            if at < EDGE:
                ready.append((EDGE - PAIR - at) // PAIR + 2)
            elif at >= EDGE + rows:
                ready.append((EDGE + 2 * rows - PAIR - at) // PAIR + 1)
            else:
                ready.append((at - EDGE) // PAIR)
        tasks.setdefault(max(ready), []).append(w // QUAD + 1)
    stages = max(max(tasks) + 1, count)
    width = 2
    for found in tasks.values():
        found.sort(key=lambda task: min(task - 1, (rows + 2 * EDGE) // QUAD - task))
    spill = max(len(found) for found in tasks.values())
    assert spill <= width and rows % QUAD == 0
    return [[(tasks.get(i, []) + [0] * width)[q] for i in range(stages)] for q in range(width)]


def convolve(sources, weight, tail, bias, target, base, group, inside):
    cols, width = target.shape[1:]
    at_col = lax.broadcasted_iota(jnp.int32, (cols, width), 0)

    def taken(rows, depths):
        return jnp.concatenate(
            [jnp.concatenate([s[base + r + d] for r in rows], axis=0) for d in depths for s in sources], axis=1
        )

    main = jnp.dot(taken(range(group), range(3)), weight[...], preferred_element_type=jnp.float32)
    rest = jnp.dot(taken(range(0, group, 2), range(4)), tail[...], preferred_element_type=jnp.float32)
    for i in range(group):
        one = main[i * cols:(i + 1) * cols]
        other = rest[i // 2 * cols:(i // 2 + 1) * cols, i % 2 * width:(i % 2 + 1) * width]
        before = jnp.where(at_col == 0, 0.0, pltpu.roll(one[:, :width], 1, 0))
        after = jnp.where(at_col == cols - 1, 0.0, pltpu.roll(other, cols - 1, 0))
        total = one[:, width:2 * width] + before + after + bias[...]
        total = jnp.maximum(total, 0.0)
        known = inside(base + i)
        if known is not None:
            total = jnp.where(known, total, 0.0)
        target[base + i] = total.astype(target.dtype)


def kernel(secs, strips, feat, offsets, w_one, b_one, w_two, b_two, w_three, out,
           mine, wide, met, corr, hid_one, hid_two, held_one, held_two, held_three, bias_one, bias_two, moved,
           main_one, rest_one, main_two, rest_two, thirds, direct_recv, relay_recv, beyond_recv, beside_recv, own_recv, send_sem, local_sem):
    rows, cols, chans = feat.shape[1:]
    hid = w_two.shape[3]
    planes = w_one.shape[2] // 2
    count = rows // PAIR
    first = count - HALO
    sec, strip = lax.axis_index("sec"), lax.axis_index("strip")
    odd = lax.rem(sec, 2)
    partner = sec + 1 - 2 * odd
    relay_to, relay_from = sec + 2 - 4 * odd, sec - 2 + 4 * odd
    has_to = (relay_to >= 0) & (relay_to < secs)
    has_from = (relay_from >= 0) & (relay_from < secs)
    has_low, has_high = strip > 0, strip < strips - 1
    core = lax.rem(strip, 2)
    beyond, beside = strip - 1 + 2 * core, strip + 1 - 2 * core
    has_beyond = (beyond >= 0) & (beyond < strips)

    barrier = pltpu.get_barrier_semaphore()
    for cond, a, b in (
        (None, partner, strip), (has_from, relay_from, strip), (None, sec, beside), (has_beyond, sec, beyond),
    ):
        when(cond, lambda a=a, b=b: pl.semaphore_signal(barrier, inc=1, device_id=(a, b), device_id_type=MESH))

    loads = [
        pltpu.make_async_copy(src, dst, local_sem.at[i])
        for i, (src, dst) in enumerate((
            (feat.at[0], mine.at[pl.ds(LEFT + STEP, rows)]), (w_one, held_one), (w_two, held_two), (w_three, held_three),
            (b_one, bias_one), (b_two, bias_two), (offsets, moved),
        ))
    ]
    for load in loads:
        load.start()
    pl.semaphore_wait(barrier, 2 + has_to.astype(jnp.int32) + has_beyond.astype(jnp.int32))

    def remote(src, dst, send, recv, a, b):
        return pltpu.make_async_remote_copy(
            src_ref=src, dst_ref=dst, send_sem=send_sem.at[send], recv_sem=recv, device_id=(a, b), device_id_type=MESH
        )

    def top_of(k):
        return jnp.where(core == 0, PAIR * k, rows - PAIR - PAIR * k)

    def direct(k):
        at = top_of(k)
        return remote(feat.at[0, pl.ds(at, PAIR)], wide.at[0, pl.ds(EDGE + at, PAIR)], 0, direct_recv.at[k], partner, strip)

    def relay(k):
        at = pl.ds(EDGE + top_of(k), PAIR)
        return remote(wide.at[0, at], wide.at[1, at], 1, relay_recv.at[k], relay_to, strip)

    def to_beyond(s, k, length):
        at = top_of(k) + core * (PAIR - length)
        to = EDGE + at + rows - 2 * rows * core
        return remote(
            wide.at[s, pl.ds(EDGE + at, length)], wide.at[s, pl.ds(to, length)], 2 + s, beyond_recv.at[s, k], sec, beyond
        )

    def to_beside(s, k, length):
        at = top_of(k) + (1 - core) * (PAIR - length)
        to = EDGE + at - rows + 2 * rows * core
        return remote(
            wide.at[s, pl.ds(EDGE + at, length)], wide.at[s, pl.ds(to, length)], 4 + s, beside_recv.at[s, k - first], sec, beside
        )

    def each_start(k, carry):
        direct(k).start()
        return carry

    lax.fori_loop(0, count, each_start, 0)
    own_low = remote(feat.at[0, pl.ds(0, STEP)], mine.at[pl.ds(LEFT + STEP + rows, STEP)], 6, own_recv.at[0], sec, strip - 1)
    own_high = remote(feat.at[0, pl.ds(rows - STEP, STEP)], mine.at[pl.ds(LEFT, STEP)], 7, own_recv.at[1], sec, strip + 1)
    when(has_low, own_low.start)
    when(has_high, own_high.start)

    zero = jnp.zeros((LEFT,) + mine.shape[1:], mine.dtype)
    mine[0:LEFT] = zero
    mine[LEFT + rows + 2 * STEP:] = zero
    for s in range(2):
        wide[s, 0] = zero[0]
        wide[s, wide.shape[1] - 1] = zero[0]

    @pl.when(jnp.logical_not(has_low))
    def _():
        mine[LEFT:LEFT + STEP] = zero[:STEP]

    @pl.when(jnp.logical_not(has_high))
    def _():
        mine[LEFT + STEP + rows:LEFT + 2 * STEP + rows] = zero[:STEP]

    @pl.when(jnp.logical_not(has_beyond))
    def _():
        for s in range(2):
            wide[s, pl.ds(core * (EDGE + rows), EDGE)] = jnp.zeros((EDGE, cols, chans), wide.dtype)

    scale = chans ** (-0.5)
    lane = lax.broadcasted_iota(jnp.int32, (cols, cols), 1)
    col = lax.broadcasted_iota(jnp.int32, (cols, cols), 0)
    other = col + lax.rem(lane, TAPS) - 4
    inside = (other >= 0) & (other < cols) & (lane < planes)
    source = lane + col - 4
    offset = lane - col + 4

    for load in loads:
        load.wait()
    for d in range(3):
        thirds[8 * d:8 * d + 8] = jnp.zeros((8, hid), thirds.dtype)
        for e in range(3):
            thirds[8 * d + 2 * e:8 * d + 2 * e + 2] = held_three[d, e].astype(thirds.dtype)
    for ref in (main_one, rest_one, rest_two):
        ref[...] = jnp.zeros(ref.shape, ref.dtype)
    for d in range(3):
        for j, place in ((0, 1 - odd), (1, odd)):
            part = pl.ds(j * planes, planes)
            at = pl.ds(pl.multiple_of((2 * d + place) * cols, cols), planes)
            next_at = pl.ds(pl.multiple_of((2 * d + 2 + place) * cols, cols), planes)
            for e in range(2):
                main_one[at, e * hid:(e + 1) * hid] = held_one[d, e, part]
            rest_one[at, 0:hid] = held_one[d, 2, part]
            rest_one[next_at, hid:2 * hid] = held_one[d, 2, part]
        at, next_at = pl.ds(d * hid, hid), pl.ds((d + 1) * hid, hid)
        for e in range(2):
            main_two[at, e * hid:(e + 1) * hid] = held_two[d, e]
        rest_two[at, 0:hid] = held_two[d, 2]
        rest_two[next_at, hid:2 * hid] = held_two[d, 2]

    when(has_low, own_high.wait_recv)
    when(has_high, own_low.wait_recv)

    below = jnp.where(sec > 0, -moved[jnp.maximum(sec - 1, 0)], 0)
    above = jnp.where(sec < secs - 1, moved[sec], 0)
    shifts = (jnp.where(odd == 1, below, above), jnp.where(odd == 1, above, below))

    def turned(s, w):
        return [pltpu.roll(wide[s, w + u], (TAPS * (w + u)) & (cols - 1), 0) for u in range(QUAD)]

    def product(own, there):
        return lax.dot_general(
            own.reshape(-1, chans), jnp.concatenate(there, axis=0), (((1,), (1,)), ((), ())),
            preferred_element_type=jnp.float32,
        )

    def shift_of(s):
        return jnp.where(s == 0, shifts[0], shifts[1])

    def full(s, w):
        there = turned(s, w)
        here = mine[pl.ds(w + LEFT - SPAN - 1 - shift_of(s), SPAN + PAIR)]
        tiles = [product(here[v * PAIR:v * PAIR + SPAN], there[v * PAIR:(v + 1) * PAIR]) for v in range(2)]

        def keep():
            place = (offset - TAPS * w) & (cols - 1)
            for j in range(SPAN + PAIR):
                us = [u for u in range(QUAD) if 0 <= TAPS - 1 - j + u < TAPS]
                kept = met[s, w + j]
                found = kept
                for u in reversed(us):
                    r = j - u // PAIR * PAIR
                    one = tiles[u // PAIR][r * cols:(r + 1) * cols, u % PAIR * cols:(u % PAIR + 1) * cols]
                    found = jnp.where(place < TAPS * (u + 1), one, found)
                if us[0] > 0:
                    found = jnp.where(place < TAPS * us[0], kept, found)
                met[s, w + j] = found

        return keep

    def edge(s, w):
        there = turned(s, w)
        begin = jnp.where(w <= QUAD, SPAN + PAIR - SHORT, 0)
        here = mine[pl.ds(w + begin + LEFT - SPAN - 1 - shift_of(s), SHORT)]
        tiles = [product(here, there[v * PAIR:(v + 1) * PAIR]) for v in range(2)]

        def keep():
            place = (offset - TAPS * w) & (cols - 1)
            for r in range(SHORT):
                j = begin + r
                low, high = TAPS * jnp.maximum(j - TAPS + 1, 0), TAPS * jnp.minimum(j + 1, QUAD)
                kept = met[s, w + j]
                found = tiles[1][r * cols:(r + 1) * cols, cols:]
                for u in reversed(range(QUAD - 1)):
                    one = tiles[u // PAIR][r * cols:(r + 1) * cols, u % PAIR * cols:(u % PAIR + 1) * cols]
                    found = jnp.where(place < TAPS * (u + 1), one, found)
                met[s, w + j] = jnp.where((place >= low) & (place < high), found, kept)

        return keep

    def meet(*steps):
        for keep in [act(s, w) for act, s, w in steps]:
            keep()

    def gather(s, e):
        index = (source + TAPS * (e + STEP + shifts[s])) & (cols - 1)
        moved_row = jnp.take_along_axis(met[s, e + SPAN + 1 + shifts[s]], index, axis=1, mode="promise_in_bounds")
        keep = inside if s == 0 else inside & has_from
        corr[s, e] = jnp.where(keep, moved_row * scale, 0.0).astype(corr.dtype)

    def gather_some(s, start, end):
        def some(g, carry):
            for i in range(BLOCK):
                gather(s, start + g * BLOCK + i)
            return carry

        lax.fori_loop(0, (end - start) // BLOCK, some, 0)

    def halo(s, at):
        k_beyond = (EDGE - PAIR - at) // PAIR
        k_beside = (EDGE + 2 * rows - PAIR - at) // PAIR
        low, high = (at < EDGE) & has_beyond, at >= EDGE + rows
        when(low & (k_beyond < HALO - 1), lambda: to_beyond(s, k_beyond, PAIR).wait_recv())
        when(low & (k_beyond == HALO - 1), lambda: to_beyond(s, k_beyond, PAIR - 1).wait_recv())
        when(high & (k_beside > first), lambda: to_beside(s, k_beside, PAIR).wait_recv())
        when(high & (k_beside == first), lambda: to_beside(s, k_beside, PAIR - 1).wait_recv())

    table = plan(rows)
    stages, width = len(table[0]), len(table)
    lone_full = any(QUAD < QUAD * (a - 1) < rows + EDGE + PAIR for a, b in zip(*table) if a > 0 and b == 0)
    codes = [sum(v << (BITS * i) for i, v in enumerate(line)) for line in table]

    def step(n, carry):
        s, j = lax.rem(n, 2), n // 2
        k = j - RELAYED * s
        known = (s == 0) | has_from

        @pl.when(known & (k >= 0) & (k < count))
        def _():
            when(s == 0, lambda: direct(k).wait_recv())
            when(s == 1, lambda: relay(k).wait_recv())
            when((s == 0) & has_to, lambda: relay(k).start())
            when(has_beyond & (k < HALO - 1), lambda: to_beyond(s, k, PAIR).start())
            when(has_beyond & (k == HALO - 1), lambda: to_beyond(s, k, PAIR - 1).start())
            when(k > first, lambda: to_beside(s, k, PAIR).start())
            when(k == first, lambda: to_beside(s, k, PAIR - 1).start())

        t = k - LATER * s

        @pl.when(known & (t >= 0) & (t < stages))
        def _():
            tasks = [lax.shift_right_logical(jnp.int32(code), BITS * t) & (2 ** BITS - 1) for code in codes]

            ws = [QUAD * (task - 1) for task in tasks]
            ats = [jnp.where(core == 0, w, rows + 2 * EDGE - QUAD - w) for w in ws]
            short = [(w <= QUAD) | (w >= rows + EDGE + PAIR) for w in ws]
            has_two = tasks[1] > 0

            @pl.when(tasks[0] > 0)
            def _():
                halo(s, ws[0])
                halo(s, ws[0] + PAIR)

            @pl.when(has_two)
            def _():
                halo(s, ws[1])
                halo(s, ws[1] + PAIR)

            alone = (tasks[0] > 0) & jnp.logical_not(has_two)
            when(alone & short[0], lambda: meet((edge, s, ats[0])))
            if lone_full:
                when(alone & jnp.logical_not(short[0]), lambda: meet((full, s, ats[0])))
            when(has_two & short[0], lambda: meet((edge, s, ats[0]), (full, s, ats[1])))
            when(has_two & jnp.logical_not(short[0]), lambda: meet((full, s, ats[0]), (full, s, ats[1])))

        when((s == 0) & (j == stages + 2), lambda: gather_some(0, 0, rows + 2 * STEP))
        return carry

    lax.fori_loop(0, (stages + RELAYED + LATER) * 2, step, 0)

    def within(margin):
        def known(r):
            if r < margin:
                return has_low
            return has_high if r >= rows + margin else None

        return known

    group = group_of(rows + 4, 4)
    ready = pl.cdiv(group + PAIR, BLOCK) * BLOCK
    gather_some(1, 0, ready)
    for base in range(0, rows + 4, group):
        for e in range(max(base + group + PAIR, ready), min(base + 2 * group + PAIR, rows + 2 * STEP)):
            gather(1, e)
        convolve((corr.at[0], corr.at[1]), main_one, rest_one, bias_one, hid_one, base, group, within(2))
    group = group_of(rows + 2, 2)
    for base in range(0, rows + 2, group):
        convolve((hid_one,), main_two, rest_two, bias_two, hid_two, base, group, within(1))

    taps = lax.dot_general(
        thirds[...].astype(hid_two.dtype), hid_two[...].reshape((rows + 2) * cols, hid), (((1,), (1,)), ((), ())),
        preferred_element_type=jnp.float32,
    )
    at_lane = lax.broadcasted_iota(jnp.int32, (8, cols), 1)
    found = []
    for r in range(rows):
        total = sum(taps[8 * d:8 * d + 8, (r + d) * cols:(r + d + 1) * cols] for d in range(3))
        before = jnp.where(at_lane == 0, 0.0, pltpu.roll(total, 1, 1))
        after = jnp.where(at_lane == cols - 1, 0.0, pltpu.roll(total, cols - 1, 1))
        found.append(before[0:2] + total[2:4] + after[4:6])
    turned = jnp.concatenate(found, axis=0)
    for r in range(rows):
        for p in range(2):
            out[p * rows + r] = turned[2 * r + p:2 * r + p + 1]

    def sent(s, length, send, a, b):
        at = pl.ds(EDGE, length)
        return remote(wide.at[s, at], wide.at[s, at], send, direct_recv.at[0], a, b).wait_send

    sent(0, rows, 0, partner, strip)()
    when(has_to, sent(0, rows, 1, relay_to, strip))
    for s, known in ((0, None), (1, has_from)):
        when(both(known, has_beyond), sent(s, SIDE, 2 + s, sec, beyond))
        when(known, sent(s, SIDE, 4 + s, sec, beside))
    when(has_low, own_low.wait_send)
    when(has_high, own_high.wait_send)


def body(secs, strips, features, offsets, state, w_first, b_first, w_second, b_second, w_third):
    _, rows, cols, chans = features.shape
    hid = w_first.shape[3]
    parts = w_third.shape[3]
    bf16 = jnp.bfloat16
    count = rows // PAIR
    thirds = jnp.transpose(w_third, (0, 1, 3, 2))
    dma = pltpu.SemaphoreType.DMA
    delta = pl.pallas_call(
        functools.partial(kernel, secs, strips),
        out_shape=jax.ShapeDtypeStruct((parts * rows, 1, cols), jnp.float32),
        in_specs=[HBM] * 7,
        out_specs=VMEM,
        scratch_shapes=[
            pltpu.VMEM((rows + 2 * STEP + 2 * LEFT, cols, chans), bf16),
            pltpu.VMEM((2, rows + 2 * EDGE, cols, chans), bf16),
            pltpu.VMEM((2, rows + 2 * EDGE + SPAN, cols, cols), jnp.float32),
            pltpu.VMEM((2, rows + 2 * STEP, cols, cols), bf16),
            pltpu.VMEM((rows + 4, cols, hid), bf16),
            pltpu.VMEM((rows + 2, cols, hid), bf16),
            pltpu.VMEM(w_first.shape, bf16),
            pltpu.VMEM(w_second.shape, bf16),
            pltpu.VMEM(thirds.shape, bf16),
            pltpu.VMEM((1, hid), jnp.float32),
            pltpu.VMEM((1, hid), jnp.float32),
            pltpu.SMEM(offsets.shape, jnp.int32),
            pltpu.VMEM((6 * cols, 2 * hid), bf16),
            pltpu.VMEM((8 * cols, 2 * hid), bf16),
            pltpu.VMEM((3 * hid, 2 * hid), bf16),
            pltpu.VMEM((4 * hid, 2 * hid), bf16),
            pltpu.VMEM((24, hid), jnp.float32),
            dma((count,)),
            dma((count,)),
            dma((2, HALO)),
            dma((2, HALO)),
            dma((2,)),
            dma((8,)),
            dma((7,)),
        ],
        compiler_params=pltpu.CompilerParams(collective_id=0, has_side_effects=True, vmem_limit_bytes=24 << 20),
    )(*(pltpu.with_memory_space_constraint(x, pltpu.HBM) for x in (features, offsets, w_first, b_first.reshape(1, hid), w_second, b_second.reshape(1, hid), thirds)))
    return state + delta.reshape(state.shape)


def solution(mesh):
    secs, strips = mesh.shape["sec"], mesh.shape["strip"]
    in_specs = (
        P("sec", "strip", None, None),
        P(),
        P(None, "sec", "strip", None),
        P(),
        P(),
        P(),
        P(),
        P(),
    )
    out_specs = P(None, "sec", "strip", None)
    return jax.shard_map(functools.partial(body, secs, strips), mesh=mesh, in_specs=in_specs, out_specs=out_specs, check_vma=False)
```

```python
import functools

import jax
import jax.numpy as jnp
from jax import lax
from jax.experimental import pallas as pl
from jax.experimental.pallas import tpu as pltpu
from jax.sharding import PartitionSpec as P

SIDE = 9
STEP = 3
PAIR = 2
TAPS = 9
SPAN = TAPS + 1
LEFT = SPAN + STEP
EDGE = SIDE + 1
HALO = EDGE // PAIR
QUAD = 2 * PAIR
RELAYED = 3
LATER = 0
SHORT = 7
BLOCK = 6
BITS = 4
HBM = pl.BlockSpec(memory_space=pltpu.HBM)
VMEM = pl.BlockSpec(memory_space=pltpu.VMEM)
MESH = pl.DeviceIdType.MESH


def group_of(rows, most):
    return max(g for g in range(2, most + 1, 2) if rows % g == 0)


def when(cond, act):
    if cond is None:
        act()
    else:
        pl.when(cond)(act)


def both(x, y):
    return y if x is None else x & y


def plan(rows):
    count = rows // PAIR
    tasks = {}
    for w in range(0, rows + 2 * EDGE, QUAD):
        ready = []
        for at in (w, w + PAIR):
            if at < EDGE:
                ready.append((EDGE - PAIR - at) // PAIR + 2)
            elif at >= EDGE + rows:
                ready.append((EDGE + 2 * rows - PAIR - at) // PAIR + 1)
            else:
                ready.append((at - EDGE) // PAIR)
        tasks.setdefault(max(ready), []).append(w // QUAD + 1)
    stages = max(max(tasks) + 1, count)
    width = 2
    for found in tasks.values():
        found.sort(key=lambda task: min(task - 1, (rows + 2 * EDGE) // QUAD - task))
    spill = max(len(found) for found in tasks.values())
    assert spill <= width and rows % QUAD == 0
    return [[(tasks.get(i, []) + [0] * width)[q] for i in range(stages)] for q in range(width)]


def convolve(sources, weight, tail, bias, target, base, group, inside):
    cols, width = target.shape[1:]
    at_col = lax.broadcasted_iota(jnp.int32, (cols, width), 0)

    def taken(rows, depths):
        return jnp.concatenate(
            [jnp.concatenate([s[base + r + d] for r in rows], axis=0) for d in depths for s in sources], axis=1
        )

    main = jnp.dot(taken(range(group), range(3)), weight[...], preferred_element_type=jnp.float32)
    rest = jnp.dot(taken(range(0, group, 2), range(4)), tail[...], preferred_element_type=jnp.float32)
    for i in range(group):
        one = main[i * cols:(i + 1) * cols]
        other = rest[i // 2 * cols:(i // 2 + 1) * cols, i % 2 * width:(i % 2 + 1) * width]
        before = jnp.where(at_col == 0, 0.0, pltpu.roll(one[:, :width], 1, 0))
        after = jnp.where(at_col == cols - 1, 0.0, pltpu.roll(other, cols - 1, 0))
        total = one[:, width:2 * width] + before + after + bias[...]
        total = jnp.maximum(total, 0.0)
        known = inside(base + i)
        if known is not None:
            total = jnp.where(known, total, 0.0)
        target[base + i] = total.astype(target.dtype)


def kernel(secs, strips, feat, offsets, w_one, b_one, w_two, b_two, w_three, out,
           mine, wide, met, corr, hid_one, hid_two, held_one, held_two, held_three, bias_one, bias_two, moved,
           main_one, rest_one, main_two, rest_two, thirds, direct_recv, relay_recv, beyond_recv, beside_recv, own_recv, send_sem, local_sem):
    rows, cols, chans = feat.shape[1:]
    hid = w_two.shape[3]
    planes = w_one.shape[2] // 2
    count = rows // PAIR
    first = count - HALO
    sec, strip = lax.axis_index("sec"), lax.axis_index("strip")
    odd = lax.rem(sec, 2)
    partner = sec + 1 - 2 * odd
    relay_to, relay_from = sec + 2 - 4 * odd, sec - 2 + 4 * odd
    has_to = (relay_to >= 0) & (relay_to < secs)
    has_from = (relay_from >= 0) & (relay_from < secs)
    has_low, has_high = strip > 0, strip < strips - 1
    core = lax.rem(strip, 2)
    beyond, beside = strip - 1 + 2 * core, strip + 1 - 2 * core
    has_beyond = (beyond >= 0) & (beyond < strips)

    barrier = pltpu.get_barrier_semaphore()
    for cond, a, b in (
        (None, partner, strip), (has_from, relay_from, strip), (None, sec, beside), (has_beyond, sec, beyond),
    ):
        when(cond, lambda a=a, b=b: pl.semaphore_signal(barrier, inc=1, device_id=(a, b), device_id_type=MESH))

    loads = [
        pltpu.make_async_copy(src, dst, local_sem.at[i])
        for i, (src, dst) in enumerate((
            (feat.at[0], mine.at[pl.ds(LEFT + STEP, rows)]), (w_one, held_one), (w_two, held_two), (w_three, held_three),
            (b_one, bias_one), (b_two, bias_two), (offsets, moved),
        ))
    ]
    for load in loads:
        load.start()
    pl.semaphore_wait(barrier, 2 + has_to.astype(jnp.int32) + has_beyond.astype(jnp.int32))

    def remote(src, dst, send, recv, a, b):
        return pltpu.make_async_remote_copy(
            src_ref=src, dst_ref=dst, send_sem=send_sem.at[send], recv_sem=recv, device_id=(a, b), device_id_type=MESH
        )

    def top_of(k):
        return jnp.where(core == 0, PAIR * k, rows - PAIR - PAIR * k)

    def direct(k):
        at = top_of(k)
        return remote(feat.at[0, pl.ds(at, PAIR)], wide.at[0, pl.ds(EDGE + at, PAIR)], 0, direct_recv.at[k], partner, strip)

    def relay(k):
        at = pl.ds(EDGE + top_of(k), PAIR)
        return remote(wide.at[0, at], wide.at[1, at], 1, relay_recv.at[k], relay_to, strip)

    def to_beyond(s, k, length):
        at = top_of(k) + core * (PAIR - length)
        to = EDGE + at + rows - 2 * rows * core
        return remote(
            wide.at[s, pl.ds(EDGE + at, length)], wide.at[s, pl.ds(to, length)], 2 + s, beyond_recv.at[s, k], sec, beyond
        )

    def to_beside(s, k, length):
        at = top_of(k) + (1 - core) * (PAIR - length)
        to = EDGE + at - rows + 2 * rows * core
        return remote(
            wide.at[s, pl.ds(EDGE + at, length)], wide.at[s, pl.ds(to, length)], 4 + s, beside_recv.at[s, k - first], sec, beside
        )

    def each_start(k, carry):
        direct(k).start()
        return carry

    lax.fori_loop(0, count, each_start, 0)
    own_low = remote(feat.at[0, pl.ds(0, STEP)], mine.at[pl.ds(LEFT + STEP + rows, STEP)], 6, own_recv.at[0], sec, strip - 1)
    own_high = remote(feat.at[0, pl.ds(rows - STEP, STEP)], mine.at[pl.ds(LEFT, STEP)], 7, own_recv.at[1], sec, strip + 1)
    when(has_low, own_low.start)
    when(has_high, own_high.start)

    zero = jnp.zeros((LEFT,) + mine.shape[1:], mine.dtype)
    mine[0:LEFT] = zero
    mine[LEFT + rows + 2 * STEP:] = zero
    for s in range(2):
        wide[s, 0] = zero[0]
        wide[s, wide.shape[1] - 1] = zero[0]

    @pl.when(jnp.logical_not(has_low))
    def _():
        mine[LEFT:LEFT + STEP] = zero[:STEP]

    @pl.when(jnp.logical_not(has_high))
    def _():
        mine[LEFT + STEP + rows:LEFT + 2 * STEP + rows] = zero[:STEP]

    @pl.when(jnp.logical_not(has_beyond))
    def _():
        for s in range(2):
            wide[s, pl.ds(core * (EDGE + rows), EDGE)] = jnp.zeros((EDGE, cols, chans), wide.dtype)

    scale = chans ** (-0.5)
    lane = lax.broadcasted_iota(jnp.int32, (cols, cols), 1)
    col = lax.broadcasted_iota(jnp.int32, (cols, cols), 0)
    other = col + lax.rem(lane, TAPS) - 4
    inside = (other >= 0) & (other < cols) & (lane < planes)
    source = lane + col - 4
    offset = lane - col + 4

    for load in loads:
        load.wait()
    for d in range(3):
        thirds[8 * d:8 * d + 8] = jnp.zeros((8, hid), thirds.dtype)
        for e in range(3):
            thirds[8 * d + 2 * e:8 * d + 2 * e + 2] = held_three[d, e].astype(thirds.dtype)
    for ref in (main_one, rest_one, rest_two):
        ref[...] = jnp.zeros(ref.shape, ref.dtype)
    for d in range(3):
        for j, place in ((0, 1 - odd), (1, odd)):
            part = pl.ds(j * planes, planes)
            at = pl.ds(pl.multiple_of((2 * d + place) * cols, cols), planes)
            next_at = pl.ds(pl.multiple_of((2 * d + 2 + place) * cols, cols), planes)
            for e in range(2):
                main_one[at, e * hid:(e + 1) * hid] = held_one[d, e, part]
            rest_one[at, 0:hid] = held_one[d, 2, part]
            rest_one[next_at, hid:2 * hid] = held_one[d, 2, part]
        at, next_at = pl.ds(d * hid, hid), pl.ds((d + 1) * hid, hid)
        for e in range(2):
            main_two[at, e * hid:(e + 1) * hid] = held_two[d, e]
        rest_two[at, 0:hid] = held_two[d, 2]
        rest_two[next_at, hid:2 * hid] = held_two[d, 2]

    when(has_low, own_high.wait_recv)
    when(has_high, own_low.wait_recv)

    below = jnp.where(sec > 0, -moved[jnp.maximum(sec - 1, 0)], 0)
    above = jnp.where(sec < secs - 1, moved[sec], 0)
    shifts = (jnp.where(odd == 1, below, above), jnp.where(odd == 1, above, below))

    def turned(s, w):
        return [pltpu.roll(wide[s, w + u], (TAPS * (w + u)) & (cols - 1), 0) for u in range(QUAD)]

    def product(own, there):
        return lax.dot_general(
            own.reshape(-1, chans), jnp.concatenate(there, axis=0), (((1,), (1,)), ((), ())),
            preferred_element_type=jnp.float32,
        )

    def shift_of(s):
        return jnp.where(s == 0, shifts[0], shifts[1])

    def full(s, w):
        there = turned(s, w)
        here = mine[pl.ds(w + LEFT - SPAN - 1 - shift_of(s), SPAN + PAIR)]
        tiles = [product(here[v * PAIR:v * PAIR + SPAN], there[v * PAIR:(v + 1) * PAIR]) for v in range(2)]

        def keep():
            place = (offset - TAPS * w) & (cols - 1)
            for j in range(SPAN + PAIR):
                us = [u for u in range(QUAD) if 0 <= TAPS - 1 - j + u < TAPS]
                kept = met[s, w + j]
                found = kept
                for u in reversed(us):
                    r = j - u // PAIR * PAIR
                    one = tiles[u // PAIR][r * cols:(r + 1) * cols, u % PAIR * cols:(u % PAIR + 1) * cols]
                    found = jnp.where(place < TAPS * (u + 1), one, found)
                if us[0] > 0:
                    found = jnp.where(place < TAPS * us[0], kept, found)
                met[s, w + j] = found

        return keep

    def edge(s, w):
        there = turned(s, w)
        begin = jnp.where(w <= QUAD, SPAN + PAIR - SHORT, 0)
        here = mine[pl.ds(w + begin + LEFT - SPAN - 1 - shift_of(s), SHORT)]
        tiles = [product(here, there[v * PAIR:(v + 1) * PAIR]) for v in range(2)]

        def keep():
            place = (offset - TAPS * w) & (cols - 1)
            for r in range(SHORT):
                j = begin + r
                low, high = TAPS * jnp.maximum(j - TAPS + 1, 0), TAPS * jnp.minimum(j + 1, QUAD)
                kept = met[s, w + j]
                found = tiles[1][r * cols:(r + 1) * cols, cols:]
                for u in reversed(range(QUAD - 1)):
                    one = tiles[u // PAIR][r * cols:(r + 1) * cols, u % PAIR * cols:(u % PAIR + 1) * cols]
                    found = jnp.where(place < TAPS * (u + 1), one, found)
                met[s, w + j] = jnp.where((place >= low) & (place < high), found, kept)

        return keep

    def meet(*steps):
        for keep in [act(s, w) for act, s, w in steps]:
            keep()

    def gather(s, e):
        index = (source + TAPS * (e + STEP + shifts[s])) & (cols - 1)
        moved_row = jnp.take_along_axis(met[s, e + SPAN + 1 + shifts[s]], index, axis=1, mode="promise_in_bounds")
        keep = inside if s == 0 else inside & has_from
        corr[s, e] = jnp.where(keep, moved_row * scale, 0.0).astype(corr.dtype)

    def gather_some(s, start, end):
        def some(g, carry):
            for i in range(BLOCK):
                gather(s, start + g * BLOCK + i)
            return carry

        lax.fori_loop(0, (end - start) // BLOCK, some, 0)

    def halo(s, at):
        k_beyond = (EDGE - PAIR - at) // PAIR
        k_beside = (EDGE + 2 * rows - PAIR - at) // PAIR
        low, high = (at < EDGE) & has_beyond, at >= EDGE + rows
        when(low & (k_beyond < HALO - 1), lambda: to_beyond(s, k_beyond, PAIR).wait_recv())
        when(low & (k_beyond == HALO - 1), lambda: to_beyond(s, k_beyond, PAIR - 1).wait_recv())
        when(high & (k_beside > first), lambda: to_beside(s, k_beside, PAIR).wait_recv())
        when(high & (k_beside == first), lambda: to_beside(s, k_beside, PAIR - 1).wait_recv())

    table = plan(rows)
    stages, width = len(table[0]), len(table)
    lone_full = any(QUAD < QUAD * (a - 1) < rows + EDGE + PAIR for a, b in zip(*table) if a > 0 and b == 0)
    codes = [sum(v << (BITS * i) for i, v in enumerate(line)) for line in table]

    def step(n, carry):
        s, j = lax.rem(n, 2), n // 2
        k = j - RELAYED * s
        known = (s == 0) | has_from

        @pl.when(known & (k >= 0) & (k < count))
        def _():
            when(s == 0, lambda: direct(k).wait_recv())
            when(s == 1, lambda: relay(k).wait_recv())
            when((s == 0) & has_to, lambda: relay(k).start())
            when(has_beyond & (k < HALO - 1), lambda: to_beyond(s, k, PAIR).start())
            when(has_beyond & (k == HALO - 1), lambda: to_beyond(s, k, PAIR - 1).start())
            when(k > first, lambda: to_beside(s, k, PAIR).start())
            when(k == first, lambda: to_beside(s, k, PAIR - 1).start())

        t = k - LATER * s

        @pl.when(known & (t >= 0) & (t < stages))
        def _():
            tasks = [lax.shift_right_logical(jnp.int32(code), BITS * t) & (2 ** BITS - 1) for code in codes]

            ws = [QUAD * (task - 1) for task in tasks]
            ats = [jnp.where(core == 0, w, rows + 2 * EDGE - QUAD - w) for w in ws]
            short = [(w <= QUAD) | (w >= rows + EDGE + PAIR) for w in ws]
            has_two = tasks[1] > 0

            @pl.when(tasks[0] > 0)
            def _():
                halo(s, ws[0])
                halo(s, ws[0] + PAIR)

            @pl.when(has_two)
            def _():
                halo(s, ws[1])
                halo(s, ws[1] + PAIR)

            alone = (tasks[0] > 0) & jnp.logical_not(has_two)
            when(alone & short[0], lambda: meet((edge, s, ats[0])))
            if lone_full:
                when(alone & jnp.logical_not(short[0]), lambda: meet((full, s, ats[0])))
            when(has_two & short[0], lambda: meet((edge, s, ats[0]), (full, s, ats[1])))
            when(has_two & jnp.logical_not(short[0]), lambda: meet((full, s, ats[0]), (full, s, ats[1])))

        when((s == 0) & (j == stages + 2), lambda: gather_some(0, 0, rows + 2 * STEP))
        return carry

    lax.fori_loop(0, (stages + RELAYED + LATER) * 2, step, 0)

    def within(margin):
        def known(r):
            if r < margin:
                return has_low
            return has_high if r >= rows + margin else None

        return known

    group = group_of(rows + 4, 2)
    ready = pl.cdiv(group + PAIR, BLOCK) * BLOCK
    gather_some(1, 0, ready)
    for base in range(0, rows + 4, group):
        for e in range(max(base + group + PAIR, ready), min(base + 2 * group + PAIR, rows + 2 * STEP)):
            gather(1, e)
        convolve((corr.at[0], corr.at[1]), main_one, rest_one, bias_one, hid_one, base, group, within(2))
    group = group_of(rows + 2, 2)
    for base in range(0, rows + 2, group):
        convolve((hid_one,), main_two, rest_two, bias_two, hid_two, base, group, within(1))

    taps = lax.dot_general(
        thirds[...].astype(hid_two.dtype), hid_two[...].reshape((rows + 2) * cols, hid), (((1,), (1,)), ((), ())),
        preferred_element_type=jnp.float32,
    )
    at_lane = lax.broadcasted_iota(jnp.int32, (8, cols), 1)
    found = []
    for r in range(rows):
        total = sum(taps[8 * d:8 * d + 8, (r + d) * cols:(r + d + 1) * cols] for d in range(3))
        before = jnp.where(at_lane == 0, 0.0, pltpu.roll(total, 1, 1))
        after = jnp.where(at_lane == cols - 1, 0.0, pltpu.roll(total, cols - 1, 1))
        found.append(before[0:2] + total[2:4] + after[4:6])
    turned = jnp.concatenate(found, axis=0)
    for r in range(rows):
        for p in range(2):
            out[p * rows + r] = turned[2 * r + p:2 * r + p + 1]

    def sent(s, length, send, a, b):
        at = pl.ds(EDGE, length)
        return remote(wide.at[s, at], wide.at[s, at], send, direct_recv.at[0], a, b).wait_send

    sent(0, rows, 0, partner, strip)()
    when(has_to, sent(0, rows, 1, relay_to, strip))
    for s, known in ((0, None), (1, has_from)):
        when(both(known, has_beyond), sent(s, SIDE, 2 + s, sec, beyond))
        when(known, sent(s, SIDE, 4 + s, sec, beside))
    when(has_low, own_low.wait_send)
    when(has_high, own_high.wait_send)


def body(secs, strips, features, offsets, state, w_first, b_first, w_second, b_second, w_third):
    _, rows, cols, chans = features.shape
    hid = w_first.shape[3]
    parts = w_third.shape[3]
    bf16 = jnp.bfloat16
    count = rows // PAIR
    thirds = jnp.transpose(w_third, (0, 1, 3, 2))
    dma = pltpu.SemaphoreType.DMA
    delta = pl.pallas_call(
        functools.partial(kernel, secs, strips),
        out_shape=jax.ShapeDtypeStruct((parts * rows, 1, cols), jnp.float32),
        in_specs=[HBM] * 7,
        out_specs=VMEM,
        scratch_shapes=[
            pltpu.VMEM((rows + 2 * STEP + 2 * LEFT, cols, chans), bf16),
            pltpu.VMEM((2, rows + 2 * EDGE, cols, chans), bf16),
            pltpu.VMEM((2, rows + 2 * EDGE + SPAN, cols, cols), jnp.float32),
            pltpu.VMEM((2, rows + 2 * STEP, cols, cols), bf16),
            pltpu.VMEM((rows + 4, cols, hid), bf16),
            pltpu.VMEM((rows + 2, cols, hid), bf16),
            pltpu.VMEM(w_first.shape, bf16),
            pltpu.VMEM(w_second.shape, bf16),
            pltpu.VMEM(thirds.shape, bf16),
            pltpu.VMEM((1, hid), jnp.float32),
            pltpu.VMEM((1, hid), jnp.float32),
            pltpu.SMEM(offsets.shape, jnp.int32),
            pltpu.VMEM((6 * cols, 2 * hid), bf16),
            pltpu.VMEM((8 * cols, 2 * hid), bf16),
            pltpu.VMEM((3 * hid, 2 * hid), bf16),
            pltpu.VMEM((4 * hid, 2 * hid), bf16),
            pltpu.VMEM((24, hid), jnp.float32),
            dma((count,)),
            dma((count,)),
            dma((2, HALO)),
            dma((2, HALO)),
            dma((2,)),
            dma((8,)),
            dma((7,)),
        ],
        compiler_params=pltpu.CompilerParams(collective_id=0, has_side_effects=True, vmem_limit_bytes=24 << 20),
    )(*(pltpu.with_memory_space_constraint(x, pltpu.HBM) for x in (features, offsets, w_first, b_first.reshape(1, hid), w_second, b_second.reshape(1, hid), thirds)))
    return state + delta.reshape(state.shape)


def solution(mesh):
    secs, strips = mesh.shape["sec"], mesh.shape["strip"]
    in_specs = (
        P("sec", "strip", None, None),
        P(),
        P(None, "sec", "strip", None),
        P(),
        P(),
        P(),
        P(),
        P(),
    )
    out_specs = P(None, "sec", "strip", None)
    return jax.shard_map(functools.partial(body, secs, strips), mesh=mesh, in_specs=in_specs, out_specs=out_specs, check_vma=False)
```
